128 devices in a mesh: seg: 32 (over y, z_hi, x), los: 4 (over z_lo, core).
Axes of the slice: x: 4, y: 4, z: 4 (z_hi: 2, z_lo: 2; z = z_hi * 2 + z_lo), core: 2. Of those that a mesh axis runs over, the one named last changes fastest.
Arguments:
- baryon_contrast: float32 [32, 128, 8192], P('seg', None, 'los'), may hold values from 0.13 to 22.2, as said below
- warmth_over_ten_thousand: float32 [32, 128, 8192], P('seg', None, 'los'), may hold values from 0.3 to 3
- peculiar_motion_shift: float32 [32, 128, 8192], P('seg', None, 'los'), may hold values from -384 to 384
- semi_extent_samples: int32 [32, 128], P(None, 'los'), may hold values from 256 to 512
- subvolume_device_lookup: int32 [32], replicated, may hold values from 0 to 31, each once
Outputs:
- flux: float32 [32, 128, 8192], P(None, 'los', 'seg')
The draws below stay inside these ranges and needn't reach their ends.
Inputs may be any that keep to these rules, and one draw needn't show every extreme that they name: `subvolume_device_lookup`: every number once. `baryon_contrast`: positive.
All inputs are finite; a program needn't handle non-finite values.
Results may differ from the reference program's by a relative error of at most 0.0003.
Values sent between devices are 32-bit elements; how exact they have to be, the bound alone decides.
A program may use at most 64 MiB of HBM per device.

```python
import math
import jax
import jax.numpy as jnp
from jax import lax

SAMPLES_IN_RAY = 8192
HALF = 512
XROWS = 1
XBLOCKS = 32
RAYS_LEADING_DIM = 32
RAYS_TRAILING_DIM = 128


def draw_baryon_contrast(key, part):
    row_frac = jnp.arange(RAYS_LEADING_DIM, dtype=jnp.float32)[:, None, None] / RAYS_LEADING_DIM
    cell_frac = jnp.arange(SAMPLES_IN_RAY, dtype=jnp.float32)[None, None, :] / SAMPLES_IN_RAY
    gradient = jnp.exp(0.5 * jnp.log(3.0) * (row_frac + cell_frac))
    normal_draw = jax.random.truncated_normal(key, -4.0, 4.0, (RAYS_LEADING_DIM, RAYS_TRAILING_DIM, SAMPLES_IN_RAY), jnp.float32)
    return jnp.exp(0.5 * normal_draw) * gradient


def draw_semi_extent_samples(key, part):
    key_values, key_high, key_low = jax.random.split(key, 3)
    values = jax.random.randint(key_values, (RAYS_LEADING_DIM * RAYS_TRAILING_DIM,), HALF // 2, HALF + 1, dtype=jnp.int32)
    high_spot = jax.random.randint(key_high, (), 0, RAYS_LEADING_DIM * RAYS_TRAILING_DIM, dtype=jnp.int32)
    low_spot = (high_spot + 1 + jax.random.randint(key_low, (), 0, RAYS_LEADING_DIM * RAYS_TRAILING_DIM - 1, dtype=jnp.int32)) % (RAYS_LEADING_DIM * RAYS_TRAILING_DIM)
    values = values.at[high_spot].set(HALF).at[low_spot].set(HALF // 2)
    return values.reshape(RAYS_LEADING_DIM, RAYS_TRAILING_DIM).astype(jnp.int32)


def block_scale(stream_key, dims, cuts, low, top_value):
    level = 1.0
    for position, parts in cuts:
        heights = jax.random.uniform(jax.random.fold_in(jax.random.fold_in(stream_key, 6), position), (parts,), jnp.float32, low / len(cuts), top_value / len(cuts))
        level = level * jnp.repeat(jnp.exp(heights), dims[position] // parts).reshape((-1,) + (1,) * (len(dims) - 1 - position))
    return level


def gaussian(stream_key, dims, width, limit, cuts=(), held_as=jnp.bfloat16):
    values = width * jax.random.normal(stream_key, dims, jnp.float32)
    if cuts:
        values = values * block_scale(stream_key, dims, cuts, -0.22, 0.18)
    return jnp.clip(values, -limit, limit).astype(held_as)


def setup_inputs(seed: int = 0) -> dict:
    key_list = jax.random.split(jax.random.key(seed), 6)
    baryon_contrast = draw_baryon_contrast(jax.random.fold_in(key_list[5], 71), 0)
    warmth_over_ten_thousand = jnp.clip(jnp.exp(math.log(3.0) - 2.3025851 * jax.random.uniform(key_list[1], (RAYS_LEADING_DIM, RAYS_TRAILING_DIM, SAMPLES_IN_RAY), jnp.float32) ** block_scale(key_list[1], (RAYS_LEADING_DIM, RAYS_TRAILING_DIM, SAMPLES_IN_RAY), ((0, 32), (2, 4)), -0.2, 0.2)), 0.3, 3.0)
    peculiar_motion_shift = gaussian(key_list[2], (RAYS_LEADING_DIM, RAYS_TRAILING_DIM, SAMPLES_IN_RAY), (HALF // 5), 384.0, ((0, 32), (2, 4)), jnp.float32)
    semi_extent_samples = draw_semi_extent_samples(jax.random.fold_in(key_list[5], 71), 0)
    subvolume_device_lookup = jax.random.permutation(key_list[4], XBLOCKS).astype(jnp.int32)
    return {"baryon_contrast": baryon_contrast, "warmth_over_ten_thousand": warmth_over_ten_thousand, "peculiar_motion_shift": peculiar_motion_shift, "semi_extent_samples": semi_extent_samples, "subvolume_device_lookup": subvolume_device_lookup}


optical_depth_normaliser = 0.3
warmth_sigma_coefficient = 13.0

def sample_local_values(baryon_contrast, warmth_over_ten_thousand, peculiar_motion_shift):
    thermal_sigma_coefficient = 1.0 / (warmth_sigma_coefficient * jnp.sqrt(warmth_over_ten_thousand))
    gaussian_contribution = optical_depth_normaliser * baryon_contrast * baryon_contrast * warmth_over_ten_thousand ** (-0.7) * thermal_sigma_coefficient
    return (gaussian_contribution, thermal_sigma_coefficient, peculiar_motion_shift)

def band_depth(gaussian_contribution, thermal_sigma_coefficient, peculiar_motion_shift, band_rows, target_width):
    target_block = math.gcd(target_width, 128)
    source_span = target_block + 2 * HALF
    row_count = gaussian_contribution.shape[0]
    offset = jnp.arange(target_block, dtype=jnp.int32)[:, None] + HALF - jnp.arange(source_span, dtype=jnp.int32)[None, :]
    inside = jnp.abs(offset)[None] <= band_rows[:, None, None]
    offset_float = offset.astype(jnp.float32)[None]

    def one_block(block_index):
        first_cell = (block_index * target_block).astype(jnp.int32)
        tile_weight = lax.dynamic_slice_in_dim(gaussian_contribution, first_cell, source_span, 1)
        tile_width = lax.dynamic_slice_in_dim(thermal_sigma_coefficient, first_cell, source_span, 1)
        tile_speed = lax.dynamic_slice_in_dim(peculiar_motion_shift, first_cell, source_span, 1)
        scaled = (offset_float - tile_speed[:, None, :]) * tile_width[:, None, :]
        contribution = jnp.where(inside, tile_weight[:, None, :] * jnp.exp(-scaled * scaled), 0.0)
        return lax.optimization_barrier(jnp.sum(contribution, axis=2))
    blocks = lax.map(one_block, jnp.arange(target_width // target_block, dtype=jnp.int32))
    return jnp.transpose(blocks, (1, 0, 2)).reshape(row_count, target_width)

def reference(baryon_contrast, warmth_over_ten_thousand, peculiar_motion_shift, semi_extent_samples, subvolume_device_lookup):
    hydro_state_bundle = sample_local_values(baryon_contrast, warmth_over_ten_thousand, peculiar_motion_shift)

    def to_box(values):
        blocks = values.reshape(XBLOCKS, XROWS, RAYS_TRAILING_DIM, SAMPLES_IN_RAY)
        return jnp.take(blocks, subvolume_device_lookup, axis=0).reshape(RAYS_LEADING_DIM * RAYS_TRAILING_DIM, SAMPLES_IN_RAY)

    def extend(values):
        return jnp.concatenate([values[:, SAMPLES_IN_RAY - HALF:], values, values[:, :HALF]], axis=1)
    extended = [extend(to_box(values)) for values in hydro_state_bundle]
    band_rows = semi_extent_samples.reshape(RAYS_LEADING_DIM * RAYS_TRAILING_DIM)
    target_width = SAMPLES_IN_RAY // 8
    group_size = math.gcd(RAYS_LEADING_DIM * RAYS_TRAILING_DIM, 16)

    def single_partition(block_number):
        first_cell = (block_number * target_width).astype(jnp.int32)

        def one_group(group_number):
            first_row = (group_number * group_size).astype(jnp.int32)
            pieces = [lax.dynamic_slice(array_in, (first_row, first_cell), (group_size, target_width + 2 * HALF)) for array_in in extended]
            band_slice = lax.dynamic_slice_in_dim(band_rows, first_row, group_size, 0)
            return band_depth(pieces[0], pieces[1], pieces[2], band_slice, target_width)
        return lax.map(one_group, jnp.arange(RAYS_LEADING_DIM * RAYS_TRAILING_DIM // group_size, dtype=jnp.int32))
    optical = lax.map(single_partition, jnp.arange(8, dtype=jnp.int32))
    optical = jnp.transpose(optical, (1, 2, 0, 3)).reshape(RAYS_LEADING_DIM * RAYS_TRAILING_DIM, SAMPLES_IN_RAY)
    flux_raw = jnp.exp(-optical)
    mean_flux = jnp.sum(flux_raw) / (RAYS_LEADING_DIM * RAYS_TRAILING_DIM * SAMPLES_IN_RAY)
    return (flux_raw / mean_flux).reshape(RAYS_LEADING_DIM, RAYS_TRAILING_DIM, SAMPLES_IN_RAY)
```

```python
import functools

import jax
import jax.numpy as jnp
from jax import lax
from jax.experimental import pallas as pl
from jax.experimental.pallas import tpu as pltpu
from jax.sharding import PartitionSpec as P

LOG2E = 1.4426950408889634
ROWS = 128
LENGTH = 2048
GROUPS = ROWS // 8
REACH = 512
SEGS, LOSS = 32, 4
WIDE = 256
CELLS = 33554432.0
MESH = pl.DeviceIdType.MESH
F32 = jnp.float32


def swap_blocks(arrays, lane):
    arrays = [list(a) for a in arrays]
    for i in range(4):
        sh = 8 << i
        bit = (lane & sh) != 0
        for m in range(16):
            if m & (1 << i):
                continue
            for v in arrays:
                a, b = v[m], v[m | (1 << i)]
                v[m] = jnp.where(bit, pltpu.roll(b, sh, 1), a)
                v[m | (1 << i)] = jnp.where(bit, b, pltpu.roll(a, 128 - sh, 1))
    return arrays


def band_kernel(perm, reach, d_ref, t_ref, v_ref, tau_ref, right_ref, left_ref, buf, W, C, NB, Q, M, Zb, S, E):
    lane = lax.broadcasted_iota(jnp.int32, (8, 128), 1)
    sub = lax.broadcasted_iota(jnp.int32, (8, 128), 0)
    gin = (lane & 7) * 16 + (lane >> 3)
    gout = (lane & 15) * 8 + (lane >> 4)
    first = lane == 0
    last = lane == 127
    zero = jnp.zeros((8, 128), F32)

    def prep(g, _):
        for i in range(8):
            y = perm[g * 8 + i]
            buf[0, pl.ds(i, 1), :] = d_ref[pl.ds(y, 1), :]
            buf[1, pl.ds(i, 1), :] = t_ref[pl.ds(y, 1), :]
            buf[2, pl.ds(i, 1), :] = v_ref[pl.ds(y, 1), :]
        dd, tt, vv = swap_blocks(
            [
                [jnp.take_along_axis(buf[n, :, m * 128 : (m + 1) * 128], gin, axis=1) for m in range(16)]
                for n in range(3)
            ],
            lane,
        )
        for t in range(16):
            C[g * 16 + t] = vv[t] + float(t)
            nb = (-LOG2E / 169.0) / tt[t]
            NB[g * 16 + t] = nb
            Q[g * 16 + t] = jnp.exp2(nb + nb)
            W[g * 16 + t] = ((0.3 / 13.0) * jnp.exp2(-1.2 * jnp.log2(tt[t]))) * (dd[t] * dd[t])
        return 0

    lax.fori_loop(0, GROUPS, prep, 0)

    zf = jnp.full((8, 128), (perm[0] >> 16).astype(F32))

    def group(g, _):
        hv = zero
        for i in range(8):
            hv = jnp.where(sub == i, reach[g * 8 + i].astype(F32), hv)
        kout = lax.div(reach[g * 8 + 7] + 15, 16)
        kin = lax.div(reach[g * 8] - 15, 16)

        def chain(ci, sign, count):
            shift = 1 if sign > 0 else 127
            hit = first if sign > 0 else last
            base = (g * 2 + ci) * 16
            for r in range(16):
                S[base + r] = zero
                E[base + r] = zero
                Zb[1, r] = zero

            def shift_up(dst):
                for r in range(16):
                    a = base + r
                    zr = pltpu.roll(S[a] + Zb[1 - dst, r], shift, 1)
                    er = pltpu.roll(E[a], shift, 1)
                    S[a] = jnp.where(hit, 0.0, zr)
                    E[a] = jnp.where(hit, zr, er)

            def cells(Z, kf, masked):
                gate = None
                for s in range(16):
                    if s % 2 == 0:
                        kb = kf if gate is None else kf + gate * zf
                    nb = NB[g * 16 + s]
                    x = kb - C[g * 16 + s]
                    m = nb * x
                    A = W[g * 16 + s] * jnp.exp2(m * x)
                    m2 = m + m
                    R = jnp.exp2(m2 + nb)
                    U = jnp.exp2(nb - m2)
                    q = Q[g * 16 + s]

                    def add(r, G):
                        term = G * M[r - s + 15] if masked else G
                        Z[r] = term if Z[r] is None else Z[r] + term

                    add(8, A)
                    G = H = A
                    for i in range(1, 9):
                        H = H * U
                        add(8 - i, H)
                        if i < 8:
                            G = G * R
                            add(8 + i, G)
                        if i < 7:
                            R = R * q
                        if i < 8:
                            U = U * q
                    gate = A

            def body(masked, n, _):
                k = kout - n
                dst = n & 1
                if masked:
                    hk = hv - (16 * k).astype(F32)
                    for i in range(31):
                        M[i] = jnp.where(hk >= float(sign * (i - 15)), 1.0, 0.0)
                Z = [None] * 16
                shift_up(dst)
                cells(Z, (sign * 16 * k + 8).astype(F32), masked)
                for r in range(16):
                    Zb[dst, r] = Z[r]
                return 0

            nm = kout - kin
            lax.fori_loop(0, nm, functools.partial(body, True), 0)
            lax.fori_loop(nm, count, functools.partial(body, False), 0)
            fin = (count - 1) & 1
            for r in range(16):
                S[base + r] = S[base + r] + Zb[fin, r]

        chain(0, 1, kout + 1)
        chain(1, -1, kout)
        return 0

    lax.fori_loop(0, GROUPS, group, 0)

    def out(g, _):
        b0 = g * 32
        b1 = b0 + 16
        tau, edge = [], []
        for r in range(16):
            zr = pltpu.roll(S[b1 + r], 127, 1)
            el = jnp.where(last, zr, pltpu.roll(E[b1 + r], 127, 1))
            tau.append(S[b0 + r] + jnp.where(last, 0.0, zr))
            edge.append(jnp.where(lane < 64, E[b0 + r], el))
        tau, edge = swap_blocks([tau, edge], lane)
        for m in range(16):
            buf[0, :, m * 128 : (m + 1) * 128] = jnp.take_along_axis(tau[m], gout, axis=1)
            if m < 4 or m >= 12:
                buf[1, :, m * 128 : (m + 1) * 128] = jnp.take_along_axis(edge[m], gout, axis=1)
        for i in range(8):
            y = perm[g * 8 + i]
            tau_ref[pl.ds(y, 1), :] = buf[0, pl.ds(i, 1), :]
            right_ref[pl.ds(y, 1), :] = buf[1, pl.ds(i, 1), 0:REACH]
            left_ref[pl.ds(y, 1), :] = buf[1, pl.ds(i, 1), LENGTH - REACH : LENGTH]
        return 0

    lax.fori_loop(0, GROUPS, out, 0)


def band_depth(perm, reach, d, t, v):
    whole = pl.BlockSpec((ROWS, LENGTH), lambda i, *_: (0, 0))
    side = pl.BlockSpec((ROWS, REACH), lambda i, *_: (0, 0))
    table = pltpu.VMEM((GROUPS * 16, 8, 128), F32)
    sums = pltpu.VMEM((GROUPS * 32, 8, 128), F32)
    return pl.pallas_call(
        band_kernel,
        out_shape=(
            jax.ShapeDtypeStruct((ROWS, LENGTH), F32),
            jax.ShapeDtypeStruct((ROWS, REACH), F32),
            jax.ShapeDtypeStruct((ROWS, REACH), F32),
        ),
        grid_spec=pltpu.PrefetchScalarGridSpec(
            num_scalar_prefetch=2,
            grid=(1,),
            in_specs=[whole] * 3,
            out_specs=[whole, side, side],
            scratch_shapes=[
                pltpu.VMEM((3, 8, LENGTH), F32),
                table,
                table,
                table,
                table,
                pltpu.VMEM((31, 8, 128), F32),
                pltpu.VMEM((2, 16, 8, 128), F32),
                sums,
                sums,
            ],
        ),
        compiler_params=pltpu.CompilerParams(vmem_limit_bytes=50 << 20),
        name="band",
    )(perm, reach, d, t, v)


def share_kernel(tau, right, left, got, sums_out, from_left, from_right, flux, part, parts, quarter, quarters,
                 edge_send, edge_recv, send, recv, sum_send, sum_recv, q_send, q_recv):
    seg, los = lax.axis_index("seg"), lax.axis_index("los")
    after, before = lax.rem(los + 1, LOSS), lax.rem(los + LOSS - 1, LOSS)
    home = lax.div(seg, 8)
    place = lax.rem(seg, 8)
    own = home == los

    barrier = pltpu.get_barrier_semaphore()

    def signal(s, l):
        pl.semaphore_signal(barrier, inc=1, device_id=(s, l), device_id_type=MESH)

    signal(seg, after)
    signal(seg, before)
    for j in range(1, 4):
        signal(lax.rem(home + j, 4) * 8 + place, los)

    def greet(s, _):
        @pl.when(jnp.logical_not(jnp.logical_and(s == seg, own)))
        def _():
            signal(s, home)
        return 0

    lax.fori_loop(0, SEGS, greet, 0)
    pl.semaphore_wait(barrier, jnp.where(own, 36, 37))

    def edge(way, block):
        rows = pl.ds(block * 32, 32)
        return pltpu.make_async_remote_copy(
            src_ref=(right if way == 0 else left).at[rows],
            dst_ref=(from_left if way == 0 else from_right).at[rows],
            send_sem=edge_send.at[way, block],
            recv_sem=edge_recv.at[way, block],
            device_id=(seg, after if way == 0 else before),
            device_id_type=MESH,
        )

    for block in range(LOSS):
        edge(0, block).start()
        edge(1, block).start()

    def piece(block, j):
        return pltpu.make_async_remote_copy(
            src_ref=flux.at[pl.ds(block * 32, 32), pl.ds(pl.multiple_of(j * WIDE, WIDE), WIDE)],
            dst_ref=got.at[seg],
            send_sem=send.at[block, j],
            recv_sem=recv.at[seg],
            device_id=(los * 8 + j, block),
            device_id_type=MESH,
        )

    def stays(block, j):
        return jnp.logical_and(los * 8 + j == seg, los == block)

    def local():
        return pltpu.make_async_copy(
            flux.at[pl.ds(pl.multiple_of(los * 32, 32), 32), pl.ds(pl.multiple_of(place * WIDE, WIDE), WIDE)],
            got.at[seg],
            recv.at[seg],
        )

    total = jnp.zeros((8, 128), F32)
    for block in range(LOSS):
        edge(0, block).wait_recv()
        edge(1, block).wait_recv()
        for sub in range(4):
            rows = pl.ds(block * 32 + sub * 8, 8)
            for m in range(16):
                cols = pl.ds(m * 128, 128)
                depth = tau[rows, cols]
                if m < 4:
                    depth = depth + from_left[rows, cols]
                if m >= 12:
                    depth = depth + from_right[rows, pl.ds((m - 12) * 128, 128)]
                value = jnp.exp(-depth)
                flux[rows, cols] = value
                total = total + value

        def ship(j, _):
            @pl.when(jnp.logical_not(stays(block, j)))
            def _():
                piece(block, j).start()
            return 0

        lax.fori_loop(0, 8, ship, 0)

    @pl.when(own)
    def _():
        local().start()

    part[...] = total

    def portion(block, j):
        return pltpu.make_async_remote_copy(
            src_ref=part,
            dst_ref=parts.at[seg],
            send_sem=sum_send.at[block, j],
            recv_sem=sum_recv.at[seg],
            device_id=(los * 8 + j, block),
            device_id_type=MESH,
        )

    def ship_sum(t, _):
        block, j = lax.div(t, 8), lax.rem(t, 8)

        @pl.when(jnp.logical_not(stays(block, j)))
        def _():
            portion(block, j).start()
        return 0

    lax.fori_loop(0, SEGS, ship_sum, 0)

    @pl.when(own)
    def _():
        parts[seg] = part[...]

    def take_sum(s, _):
        @pl.when(jnp.logical_not(jnp.logical_and(s == seg, own)))
        def _():
            pltpu.make_async_remote_copy(
                src_ref=part, dst_ref=parts.at[s], send_sem=sum_send.at[0, 0], recv_sem=sum_recv.at[s],
                device_id=(s, home), device_id_type=MESH,
            ).wait_recv()
        return 0

    lax.fori_loop(0, SEGS, take_sum, 0)
    mine = parts[0]
    for s in range(1, SEGS):
        mine = mine + parts[s]
    quarter[...] = mine

    def swap(j):
        return pltpu.make_async_remote_copy(
            src_ref=quarter,
            dst_ref=quarters.at[j - 1],
            send_sem=q_send.at[j - 1],
            recv_sem=q_recv.at[j - 1],
            device_id=(lax.rem(home + j, 4) * 8 + place, los),
            device_id_type=MESH,
        )

    for j in range(1, 4):
        swap(j).start()
    for j in range(1, 4):
        swap(j).wait_recv()
    sums_out[...] = mine + quarters[0] + quarters[1] + quarters[2]

    def take(s, _):
        @pl.when(jnp.logical_not(jnp.logical_and(s == seg, own)))
        def _():
            pltpu.make_async_remote_copy(
                src_ref=flux.at[pl.ds(0, 32), pl.ds(0, WIDE)], dst_ref=got.at[s], send_sem=send.at[0, 0],
                recv_sem=recv.at[s], device_id=(s, home), device_id_type=MESH,
            ).wait_recv()
        return 0

    lax.fori_loop(0, SEGS, take, 0)

    @pl.when(own)
    def _():
        local().wait()

    for block in range(LOSS):
        edge(0, block).wait_send()
        edge(1, block).wait_send()

    def sent(t, _):
        block, j = lax.div(t, 8), lax.rem(t, 8)

        @pl.when(jnp.logical_not(stays(block, j)))
        def _():
            piece(block, j).wait_send()
            portion(block, j).wait_send()
        return 0

    lax.fori_loop(0, SEGS, sent, 0)
    for j in range(1, 4):
        swap(j).wait_send()


def share(tau, right, left):
    vmem = pl.BlockSpec(memory_space=pltpu.VMEM)
    dma = pltpu.SemaphoreType.DMA
    return pl.pallas_call(
        share_kernel,
        out_shape=(jax.ShapeDtypeStruct((SEGS, 32, WIDE), F32), jax.ShapeDtypeStruct((8, 128), F32)),
        in_specs=[vmem] * 3,
        out_specs=(pl.BlockSpec(memory_space=pl.ANY), vmem),
        scratch_shapes=[
            pltpu.VMEM((ROWS, REACH), F32),
            pltpu.VMEM((ROWS, REACH), F32),
            pltpu.VMEM((ROWS, LENGTH), F32),
            pltpu.VMEM((8, 128), F32),
            pltpu.VMEM((SEGS, 8, 128), F32),
            pltpu.VMEM((8, 128), F32),
            pltpu.VMEM((3, 8, 128), F32),
            dma((2, LOSS)),
            dma((2, LOSS)),
            dma((LOSS, 8)),
            dma((SEGS,)),
            dma((LOSS, 8)),
            dma((SEGS,)),
            dma((3,)),
            dma((3,)),
        ],
        compiler_params=pltpu.CompilerParams(collective_id=0, has_side_effects=True, vmem_limit_bytes=24 << 20),
        name="share",
    )(tau, right, left)


def per_device(contrast, warmth, velocity, semi_extent, lookup):
    seg = lax.axis_index("seg")
    mine = lookup == seg
    own = jnp.sum(jnp.where(mine[:, None], semi_extent, 0).astype(F32), axis=0)
    h = lax.all_gather(own, "los", tiled=True)
    at = jnp.arange(ROWS)
    below = (h[None, :] < h[:, None]) | ((h[None, :] == h[:, None]) & (at[None, :] < at[:, None]))
    rank = jnp.sum(below.astype(jnp.int32), axis=1)
    hot = rank[:, None] == at[None, :]
    perm = jnp.sum(jnp.where(hot, at[:, None], 0), axis=0).astype(jnp.int32)
    reach = jnp.sum(jnp.where(hot, h[:, None], 0.0), axis=0).astype(jnp.int32)
    shape = (ROWS, LENGTH)
    tau, right, left = band_depth(
        perm, reach, contrast.reshape(shape), warmth.reshape(shape), velocity.reshape(shape)
    )
    got, sums = share(tau, right, left)
    scale = CELLS / jnp.sum(sums)
    return jnp.take(got, lookup, axis=0) * scale


def solution(mesh):
    return jax.shard_map(
        per_device,
        mesh=mesh,
        in_specs=(P("seg", None, "los"), P("seg", None, "los"), P("seg", None, "los"), P(None, "los"), P()),
        out_specs=P(None, "los", "seg"),
        check_vma=False,
    )
```

```python
import functools

import jax
import jax.numpy as jnp
from jax import lax
from jax.experimental import pallas as pl
from jax.experimental.pallas import tpu as pltpu
from jax.sharding import PartitionSpec as P

LOG2E = 1.4426950408889634
ROWS = 128
LENGTH = 2048
GROUPS = ROWS // 8
REACH = 512
SEGS, LOSS = 32, 4
WIDE = 256
CELLS = 33554432.0
MESH = pl.DeviceIdType.MESH
F32 = jnp.float32


def swap_blocks(arrays, lane):
    arrays = [list(a) for a in arrays]
    for i in range(4):
        sh = 8 << i
        bit = (lane & sh) != 0
        for m in range(16):
            if m & (1 << i):
                continue
            for v in arrays:
                a, b = v[m], v[m | (1 << i)]
                v[m] = jnp.where(bit, pltpu.roll(b, sh, 1), a)
                v[m | (1 << i)] = jnp.where(bit, b, pltpu.roll(a, 128 - sh, 1))
    return arrays


def band_kernel(perm, reach, d_ref, t_ref, v_ref, tau_ref, right_ref, left_ref, buf, W, C, NB, Q, M, Zb, S, E):
    lane = lax.broadcasted_iota(jnp.int32, (8, 128), 1)
    sub = lax.broadcasted_iota(jnp.int32, (8, 128), 0)
    gin = (lane & 7) * 16 + (lane >> 3)
    gout = (lane & 15) * 8 + (lane >> 4)
    first = lane == 0
    last = lane == 127
    zero = jnp.zeros((8, 128), F32)

    def prep(g, _):
        for i in range(8):
            y = perm[g * 8 + i]
            buf[0, pl.ds(i, 1), :] = d_ref[pl.ds(y, 1), :]
            buf[1, pl.ds(i, 1), :] = t_ref[pl.ds(y, 1), :]
            buf[2, pl.ds(i, 1), :] = v_ref[pl.ds(y, 1), :]
        dd, tt, vv = swap_blocks(
            [
                [jnp.take_along_axis(buf[n, :, m * 128 : (m + 1) * 128], gin, axis=1) for m in range(16)]
                for n in range(3)
            ],
            lane,
        )
        for t in range(16):
            C[g * 16 + t] = vv[t] + float(t)
            nb = (-LOG2E / 169.0) / tt[t]
            NB[g * 16 + t] = nb
            Q[g * 16 + t] = jnp.exp2(nb + nb)
            W[g * 16 + t] = ((0.3 / 13.0) * jnp.exp2(-1.2 * jnp.log2(tt[t]))) * (dd[t] * dd[t])
        return 0

    lax.fori_loop(0, GROUPS, prep, 0)

    zf = jnp.full((8, 128), (perm[0] >> 16).astype(F32))

    def group(g, _):
        hv = zero
        for i in range(8):
            hv = jnp.where(sub == i, reach[g * 8 + i].astype(F32), hv)
        kout = lax.div(reach[g * 8 + 7] + 15, 16)
        kin = lax.div(reach[g * 8] - 15, 16)

        def chain(ci, sign, count):
            shift = 1 if sign > 0 else 127
            hit = first if sign > 0 else last
            base = (g * 2 + ci) * 16
            for r in range(16):
                S[base + r] = zero
                E[base + r] = zero
                Zb[1, r] = zero

            def shift_up(dst):
                for r in range(16):
                    a = base + r
                    zr = pltpu.roll(S[a] + Zb[1 - dst, r], shift, 1)
                    er = pltpu.roll(E[a], shift, 1)
                    S[a] = jnp.where(hit, 0.0, zr)
                    E[a] = jnp.where(hit, zr, er)

            def cells(Z, kf, masked):
                gate = None
                for s in range(16):
                    if s % 2 == 0:
                        kb = kf if gate is None else kf + gate * zf
                    nb = NB[g * 16 + s]
                    x = kb - C[g * 16 + s]
                    m = nb * x
                    A = W[g * 16 + s] * jnp.exp2(m * x)
                    m2 = m + m
                    R = jnp.exp2(m2 + nb)
                    U = jnp.exp2(nb - m2)
                    q = Q[g * 16 + s]

                    def add(r, G):
                        term = G * M[r - s + 15] if masked else G
                        Z[r] = term if Z[r] is None else Z[r] + term

                    add(8, A)
                    G = H = A
                    for i in range(1, 9):
                        H = H * U
                        add(8 - i, H)
                        if i < 8:
                            G = G * R
                            add(8 + i, G)
                        if i < 7:
                            R = R * q
                        if i < 8:
                            U = U * q
                    gate = A

            def body(masked, n, _):
                k = kout - n
                dst = n & 1
                if masked:
                    hk = hv - (16 * k).astype(F32)
                    for i in range(31):
                        M[i] = jnp.where(hk >= float(sign * (i - 15)), 1.0, 0.0)
                Z = [None] * 16
                shift_up(dst)
                cells(Z, (sign * 16 * k + 8).astype(F32), masked)
                for r in range(16):
                    Zb[dst, r] = Z[r]
                return 0

            nm = kout - kin
            lax.fori_loop(0, nm, functools.partial(body, True), 0)
            lax.fori_loop(nm, count, functools.partial(body, False), 0)
            fin = (count - 1) & 1
            for r in range(16):
                S[base + r] = S[base + r] + Zb[fin, r]

        chain(0, 1, kout + 1)
        chain(1, -1, kout)
        return 0

    lax.fori_loop(0, GROUPS, group, 0)

    def out(g, _):
        b0 = g * 32
        b1 = b0 + 16
        tau, edge = [], []
        for r in range(16):
            zr = pltpu.roll(S[b1 + r], 127, 1)
            el = jnp.where(last, zr, pltpu.roll(E[b1 + r], 127, 1))
            tau.append(S[b0 + r] + jnp.where(last, 0.0, zr))
            edge.append(jnp.where(lane < 64, E[b0 + r], el))
        tau, edge = swap_blocks([tau, edge], lane)
        for m in range(16):
            buf[0, :, m * 128 : (m + 1) * 128] = jnp.take_along_axis(tau[m], gout, axis=1)
            if m < 4 or m >= 12:
                buf[1, :, m * 128 : (m + 1) * 128] = jnp.take_along_axis(edge[m], gout, axis=1)
        for i in range(8):
            y = perm[g * 8 + i]
            tau_ref[pl.ds(y, 1), :] = buf[0, pl.ds(i, 1), :]
            right_ref[pl.ds(y, 1), :] = buf[1, pl.ds(i, 1), 0:REACH]
            left_ref[pl.ds(y, 1), :] = buf[1, pl.ds(i, 1), LENGTH - REACH : LENGTH]
        return 0

    lax.fori_loop(0, GROUPS, out, 0)


def band_depth(perm, reach, d, t, v):
    whole = pl.BlockSpec((ROWS, LENGTH), lambda i, *_: (0, 0))
    side = pl.BlockSpec((ROWS, REACH), lambda i, *_: (0, 0))
    table = pltpu.VMEM((GROUPS * 16, 8, 128), F32)
    sums = pltpu.VMEM((GROUPS * 32, 8, 128), F32)
    return pl.pallas_call(
        band_kernel,
        out_shape=(
            jax.ShapeDtypeStruct((ROWS, LENGTH), F32),
            jax.ShapeDtypeStruct((ROWS, REACH), F32),
            jax.ShapeDtypeStruct((ROWS, REACH), F32),
        ),
        grid_spec=pltpu.PrefetchScalarGridSpec(
            num_scalar_prefetch=2,
            grid=(1,),
            in_specs=[whole] * 3,
            out_specs=[whole, side, side],
            scratch_shapes=[
                pltpu.VMEM((3, 8, LENGTH), F32),
                table,
                table,
                table,
                table,
                pltpu.VMEM((31, 8, 128), F32),
                pltpu.VMEM((2, 16, 8, 128), F32),
                sums,
                sums,
            ],
        ),
        compiler_params=pltpu.CompilerParams(vmem_limit_bytes=50 << 20),
        name="band",
    )(perm, reach, d, t, v)


def share_kernel(tau, right, left, got, sums_out, from_left, from_right, flux, relay, part, parts, local_sum, sums,
                 edge_send, edge_recv, a_send, a_recv, b_send, b_recv, p_send, p_recv, q_send, q_recv):
    seg, los = lax.axis_index("seg"), lax.axis_index("los")
    y, zh, x = lax.div(seg, 8), lax.rem(lax.div(seg, 4), 2), lax.rem(seg, 4)
    zl, core = lax.div(los, 2), lax.rem(los, 2)
    after, before = lax.rem(los + 1, LOSS), lax.rem(los + LOSS - 1, LOSS)
    me = zh * 4 + los

    def column(d):
        h = 1 - zh if d & 4 else zh
        l = (1 - zl if d & 2 else zl) * 2 + (1 - core if d & 1 else core)
        return h, l

    def plane(dy, dx):
        return lax.rem(y + dy, 4) * 8 + zh * 4 + lax.rem(x + dx, 4)

    barrier = pltpu.get_barrier_semaphore()

    def signal(s, l):
        pl.semaphore_signal(barrier, inc=1, device_id=(s, l), device_id_type=MESH)

    for d in range(1, 8):
        h, l = column(d)
        signal(y * 8 + h * 4 + x, l)
    for i in range(1, 16):
        signal(plane(i // 4, i % 4), los)
    pl.semaphore_wait(barrier, 22)

    def remote(src, dst, send, recv, s, l):
        return pltpu.make_async_remote_copy(
            src_ref=src, dst_ref=dst, send_sem=send, recv_sem=recv, device_id=(s, l), device_id_type=MESH
        )

    edges = [
        remote(right, from_left, edge_send.at[0], edge_recv.at[0], seg, after),
        remote(left, from_right, edge_send.at[1], edge_recv.at[1], seg, before),
    ]
    for copy in edges:
        copy.start()
    for copy in edges:
        copy.wait_recv()

    def rows_of(i, total):
        rows = pl.ds(pl.multiple_of(i * 8, 8), 8)
        for m in range(16):
            cols = pl.ds(m * 128, 128)
            depth = tau[rows, cols]
            if m < 4:
                depth = depth + from_left[rows, cols]
            if m >= 12:
                depth = depth + from_right[rows, pl.ds((m - 12) * 128, 128)]
            value = jnp.exp(-depth)
            flux[rows, cols] = value
            total = total + value
        return total

    part[...] = lax.fori_loop(0, GROUPS, rows_of, jnp.zeros((8, 128), F32))

    def a_part(d):
        h, l = column(d)
        return flux.at[pl.ds(pl.multiple_of(l * 32, 32), 32), pl.ds(pl.multiple_of(h * 1024, 1024), 1024)]

    def a_copy(d):
        h, l = column(d)
        return remote(a_part(d), relay.at[me], a_send.at[d], a_recv.at[me], y * 8 + h * 4 + x, l)

    def a_arrival(d):
        h, l = column(d)
        return remote(a_part(d), relay.at[h * 4 + l], a_send.at[d], a_recv.at[h * 4 + l], y * 8 + h * 4 + x, l)

    def p_copy(d):
        h, l = column(d)
        return remote(part, parts.at[d - 1], p_send.at[d - 1], p_recv.at[d - 1], y * 8 + h * 4 + x, l)

    for d in range(1, 8):
        p_copy(d).start()
    keep = pltpu.make_async_copy(a_part(0), relay.at[me], a_recv.at[me])
    for d in (4, 2, 6, 5, 3, 7, 1):
        a_copy(d).start()
    keep.start()

    total = part[...]
    for d in range(1, 8):
        p_copy(d).wait_recv()
        total = total + parts[d - 1]
    local_sum[...] = total

    def q_copy(i):
        return remote(local_sum, sums.at[i - 1], q_send.at[i - 1], q_recv.at[i - 1], plane(i // 4, i % 4), los)

    for i in range(1, 16):
        q_copy(i).start()

    def b_part(d, j):
        h, l = column(d)
        to = lax.rem(x + j, 4)
        return relay.at[h * 4 + l, :, pl.ds(pl.multiple_of(to * WIDE, WIDE), WIDE)]

    def b_copy(d, j):
        h, l = column(d)
        slot = y * 8 + h * 4 + x
        return remote(b_part(d, j), got.at[slot], b_send.at[d, j], b_recv.at[slot],
                      l * 8 + zh * 4 + lax.rem(x + j, 4), los)

    def b_keep(d):
        h, l = column(d)
        slot = y * 8 + h * 4 + x
        return pltpu.make_async_copy(b_part(d, 0), got.at[slot], b_recv.at[slot])

    def stays(d):
        return column(d)[1] == y

    def leaves(d):
        return column(d)[1] != y

    for d in (0, 1, 2, 6, 3, 7, 4, 5):
        if d == 0:
            keep.wait()
        else:
            a_arrival(d).wait_recv()
        for j in (2, 1, 3):
            b_copy(d, j).start()

        @pl.when(leaves(d))
        def _():
            b_copy(d, 0).start()

        @pl.when(stays(d))
        def _():
            b_keep(d).start()

    for i in range(1, 16):
        q_copy(i).wait_recv()
        total = total + sums[i - 1]
    sums_out[...] = total

    def take(s, _):
        ys, xs = lax.div(s, 8), lax.rem(s, 4)
        here = jnp.logical_and(ys == y, xs == x)

        @pl.when(jnp.logical_not(here))
        def _():
            remote(relay.at[0, :, pl.ds(0, WIDE)], got.at[s], b_send.at[0, 1], b_recv.at[s],
                   ys * 8 + zh * 4 + xs, los).wait_recv()

        @pl.when(here)
        def _():
            pltpu.make_async_copy(relay.at[0, :, pl.ds(0, WIDE)], got.at[s], b_recv.at[s]).wait()
        return 0

    lax.fori_loop(0, SEGS, take, 0)

    for copy in edges:
        copy.wait_send()
    for d in range(1, 8):
        a_copy(d).wait_send()
        p_copy(d).wait_send()
    for i in range(1, 16):
        q_copy(i).wait_send()
    for d in range(8):
        for j in (1, 2, 3):
            b_copy(d, j).wait_send()

        @pl.when(leaves(d))
        def _():
            b_copy(d, 0).wait_send()


def share(tau, right, left):
    vmem = pl.BlockSpec(memory_space=pltpu.VMEM)
    dma = pltpu.SemaphoreType.DMA
    return pl.pallas_call(
        share_kernel,
        out_shape=(jax.ShapeDtypeStruct((SEGS, 32, WIDE), F32), jax.ShapeDtypeStruct((8, 128), F32)),
        in_specs=[vmem] * 3,
        out_specs=(pl.BlockSpec(memory_space=pl.ANY), vmem),
        scratch_shapes=[
            pltpu.VMEM((ROWS, REACH), F32),
            pltpu.VMEM((ROWS, REACH), F32),
            pltpu.VMEM((ROWS, LENGTH), F32),
            pltpu.VMEM((8, 32, 1024), F32),
            pltpu.VMEM((8, 128), F32),
            pltpu.VMEM((7, 8, 128), F32),
            pltpu.VMEM((8, 128), F32),
            pltpu.VMEM((15, 8, 128), F32),
            dma((2,)),
            dma((2,)),
            dma((8,)),
            dma((8,)),
            dma((8, 4)),
            dma((SEGS,)),
            dma((7,)),
            dma((7,)),
            dma((15,)),
            dma((15,)),
        ],
        compiler_params=pltpu.CompilerParams(collective_id=0, has_side_effects=True, vmem_limit_bytes=24 << 20),
        name="share",
    )(tau, right, left)


def per_device(contrast, warmth, velocity, semi_extent, lookup):
    seg = lax.axis_index("seg")
    mine = lookup == seg
    own = jnp.sum(jnp.where(mine[:, None], semi_extent, 0).astype(F32), axis=0)
    h = lax.all_gather(own, "los", tiled=True)
    at = jnp.arange(ROWS)
    below = (h[None, :] < h[:, None]) | ((h[None, :] == h[:, None]) & (at[None, :] < at[:, None]))
    rank = jnp.sum(below.astype(jnp.int32), axis=1)
    hot = rank[:, None] == at[None, :]
    perm = jnp.sum(jnp.where(hot, at[:, None], 0), axis=0).astype(jnp.int32)
    reach = jnp.sum(jnp.where(hot, h[:, None], 0.0), axis=0).astype(jnp.int32)
    shape = (ROWS, LENGTH)
    tau, right, left = band_depth(
        perm, reach, contrast.reshape(shape), warmth.reshape(shape), velocity.reshape(shape)
    )
    got, sums = share(tau, right, left)
    scale = CELLS / jnp.sum(sums)
    return jnp.take(got, lookup, axis=0) * scale


def solution(mesh):
    return jax.shard_map(
        per_device,
        mesh=mesh,
        in_specs=(P("seg", None, "los"), P("seg", None, "los"), P("seg", None, "los"), P(None, "los"), P()),
        out_specs=P(None, "los", "seg"),
        check_vma=False,
    )
```

```python
import functools

import jax
import jax.numpy as jnp
from jax import lax
from jax.experimental import pallas as pl
from jax.experimental.pallas import tpu as pltpu
from jax.sharding import PartitionSpec as P

LOG2E = 1.4426950408889634
ROWS = 128
LENGTH = 2048
GROUPS = ROWS // 8
REACH = 512
SEGS, LOSS = 32, 4
WIDE = 256
CELLS = 33554432.0
MESH = pl.DeviceIdType.MESH
F32 = jnp.float32


def band_kernel(perm, reach, d_ref, t_ref, v_ref, tau_ref, edge_ref, W, C, NB, Q, M, Zb, S, E):
    lane = lax.broadcasted_iota(jnp.int32, (8, 128), 1)
    sub = lax.broadcasted_iota(jnp.int32, (8, 128), 0)
    zero = jnp.zeros((8, 128), F32)

    def gather(g, _):
        at = pl.ds(pl.multiple_of(g * 16, 16), 16)
        for i in range(8):
            y = perm[g * 8 + i]
            W[at, i : i + 1, :] = d_ref[:, pl.ds(y, 1), :]
            NB[at, i : i + 1, :] = t_ref[:, pl.ds(y, 1), :]
            C[at, i : i + 1, :] = v_ref[:, pl.ds(y, 1), :]
        return 0

    lax.fori_loop(0, GROUPS, gather, 0)

    def prep(g, _):
        for t in range(16):
            a = g * 16 + t
            warmth = NB[a]
            contrast = W[a]
            nb = (-LOG2E / 169.0) / warmth
            C[a] = C[a] + float(t)
            NB[a] = nb
            Q[a] = jnp.exp2(nb + nb)
            W[a] = ((0.3 / 13.0) * jnp.exp2(-1.2 * jnp.log2(warmth))) * (contrast * contrast)
            S[a] = zero
            E[a] = zero
        return 0

    lax.fori_loop(0, GROUPS, prep, 0)

    def group(g, _):
        hv = zero
        for i in range(8):
            hv = jnp.where(sub == i, reach[g * 8 + i].astype(F32), hv)
        kout = lax.div(reach[g * 8 + 7] + 15, 16)
        kin = lax.div(reach[g * 8] - 15, 16)
        base = g * 16
        for r in range(16):
            Zb[1, r] = zero

        def place(dst, sk):
            shift = lax.rem(sk + 128, 128)
            inside = jnp.logical_and(lane >= sk, lane < sk + 128)
            for r in range(16):
                z = pltpu.roll(Zb[1 - dst, r], shift, 1)
                S[base + r] = S[base + r] + jnp.where(inside, z, 0.0)
                E[base + r] = E[base + r] + jnp.where(inside, 0.0, z)

        def cells(Z, kf, masked):
            for s in range(16):
                nb = NB[base + s]
                x = kf - C[base + s]
                m = nb * x
                A = W[base + s] * jnp.exp2(m * x)
                m2 = m + m
                R = jnp.exp2(m2 + nb)
                U = jnp.exp2(nb - m2)
                q = Q[base + s]

                def add(r, G):
                    term = G * M[r - s + 15] if masked else G
                    Z[r] = term if Z[r] is None else Z[r] + term

                add(8, A)
                G = H = A
                for i in range(1, 9):
                    H = H * U
                    add(8 - i, H)
                    if i < 8:
                        G = G * R
                        add(8 + i, G)
                    if i < 7:
                        R = R * q
                    if i < 8:
                        U = U * q

        def body(side, where, n, carry):
            before, dst = carry
            sk = where(n)
            if side:
                hk = hv - (16 * side * sk).astype(F32)
                for i in range(31):
                    M[i] = jnp.where(hk >= float(side * (i - 15)), 1.0, 0.0)
            Z = [None] * 16
            place(dst, before)
            cells(Z, (16 * sk + 8).astype(F32), side)
            for r in range(16):
                Zb[dst, r] = Z[r]
            return sk, 1 - dst

        carry = (jnp.int32(0), jnp.int32(0))
        carry = lax.fori_loop(0, kout - kin, functools.partial(body, -1, lambda n: n - kout), carry)
        carry = lax.fori_loop(0, kout - kin, functools.partial(body, 1, lambda n: kout - n), carry)
        carry = lax.fori_loop(
            0, 2 * kin + 1, functools.partial(body, 0, lambda n: jnp.where(n < kin, n - kin, 2 * kin - n)), carry
        )
        fin = 1 - carry[1]
        for r in range(16):
            S[base + r] = S[base + r] + Zb[fin, r]
        return 0

    lax.fori_loop(0, GROUPS, group, 0)

    def scatter(g, _):
        at = pl.ds(pl.multiple_of(g * 16, 16), 16)
        for i in range(8):
            y = perm[g * 8 + i]
            tau_ref[:, pl.ds(y, 1), :] = S[at, i : i + 1, :]
            edge_ref[:, pl.ds(y, 1), :] = E[at, i : i + 1, :]
        return 0

    lax.fori_loop(0, GROUPS, scatter, 0)

def band_depth(perm, reach, d, t, v):
    whole = pl.BlockSpec((16, ROWS, 128), lambda i, *_: (0, 0, 0))
    table = pltpu.VMEM((GROUPS * 16, 8, 128), F32)
    return pl.pallas_call(
        band_kernel,
        out_shape=(jax.ShapeDtypeStruct((16, ROWS, 128), F32),) * 2,
        grid_spec=pltpu.PrefetchScalarGridSpec(
            num_scalar_prefetch=2, grid=(1,), in_specs=[whole] * 3, out_specs=[whole] * 2,
            scratch_shapes=[table] * 4 + [pltpu.VMEM((31, 8, 128), F32), pltpu.VMEM((2, 16, 8, 128), F32), table, table],
        ),
        compiler_params=pltpu.CompilerParams(vmem_limit_bytes=40 << 20),
        name="band",
    )(perm, reach, d, t, v)


def share_kernel(tau, right, left, got, sums_out, from_left, from_right, flux, relay, part, parts, local_sum, sums,
                 edge_send, edge_recv, a_send, a_recv, b_send, b_recv, p_send, p_recv, q_send, q_recv):
    seg, los = lax.axis_index("seg"), lax.axis_index("los")
    y, zh, x = lax.div(seg, 8), lax.rem(lax.div(seg, 4), 2), lax.rem(seg, 4)
    zl, core = lax.div(los, 2), lax.rem(los, 2)
    after, before = lax.rem(los + 1, LOSS), lax.rem(los + LOSS - 1, LOSS)
    me = zh * 4 + los

    def column(d):
        h = 1 - zh if d & 4 else zh
        l = (1 - zl if d & 2 else zl) * 2 + (1 - core if d & 1 else core)
        return h, l

    def plane(dy, dx):
        return lax.rem(y + dy, 4) * 8 + zh * 4 + lax.rem(x + dx, 4)

    barrier = pltpu.get_barrier_semaphore()

    def signal(s, l):
        pl.semaphore_signal(barrier, inc=1, device_id=(s, l), device_id_type=MESH)

    for d in range(1, 8):
        h, l = column(d)
        signal(y * 8 + h * 4 + x, l)
    for i in range(1, 16):
        signal(plane(i // 4, i % 4), los)
    pl.semaphore_wait(barrier, 22)

    def remote(src, dst, send, recv, s, l):
        return pltpu.make_async_remote_copy(
            src_ref=src, dst_ref=dst, send_sem=send, recv_sem=recv, device_id=(s, l), device_id_type=MESH
        )

    edges = [
        remote(right, from_left, edge_send.at[0], edge_recv.at[0], seg, after),
        remote(left, from_right, edge_send.at[1], edge_recv.at[1], seg, before),
    ]
    for copy in edges:
        copy.start()
    for copy in edges:
        copy.wait_recv()

    def rows_of(i, total):
        rows = pl.ds(pl.multiple_of(i * 8, 8), 8)
        for m in range(16):
            cols = pl.ds(m * 128, 128)
            depth = tau[rows, cols]
            if m < 4:
                depth = depth + from_left[rows, cols]
            if m >= 12:
                depth = depth + from_right[rows, pl.ds((m - 12) * 128, 128)]
            value = jnp.exp(-depth)
            flux[rows, cols] = value
            total = total + value
        return total

    part[...] = lax.fori_loop(0, GROUPS, rows_of, jnp.zeros((8, 128), F32))

    def a_part(d):
        h, l = column(d)
        return flux.at[pl.ds(pl.multiple_of(l * 32, 32), 32), pl.ds(pl.multiple_of(h * 1024, 1024), 1024)]

    def a_copy(d):
        h, l = column(d)
        return remote(a_part(d), relay.at[me], a_send.at[d], a_recv.at[me], y * 8 + h * 4 + x, l)

    def a_arrival(d):
        h, l = column(d)
        return remote(a_part(d), relay.at[h * 4 + l], a_send.at[d], a_recv.at[h * 4 + l], y * 8 + h * 4 + x, l)

    def p_copy(d):
        h, l = column(d)
        return remote(part, parts.at[d - 1], p_send.at[d - 1], p_recv.at[d - 1], y * 8 + h * 4 + x, l)

    for d in range(1, 8):
        p_copy(d).start()
    keep = pltpu.make_async_copy(a_part(0), relay.at[me], a_recv.at[me])
    for d in (4, 2, 6, 5, 3, 7, 1):
        a_copy(d).start()
    keep.start()

    total = part[...]
    for d in range(1, 8):
        p_copy(d).wait_recv()
        total = total + parts[d - 1]
    local_sum[...] = total

    def q_copy(i):
        return remote(local_sum, sums.at[i - 1], q_send.at[i - 1], q_recv.at[i - 1], plane(i // 4, i % 4), los)

    for i in range(1, 16):
        q_copy(i).start()

    def b_part(d, j):
        h, l = column(d)
        to = lax.rem(x + j, 4)
        return relay.at[h * 4 + l, :, pl.ds(pl.multiple_of(to * WIDE, WIDE), WIDE)]

    def b_copy(d, j):
        h, l = column(d)
        slot = y * 8 + h * 4 + x
        return remote(b_part(d, j), got.at[slot], b_send.at[d, j], b_recv.at[slot],
                      l * 8 + zh * 4 + lax.rem(x + j, 4), los)

    def b_keep(d):
        h, l = column(d)
        slot = y * 8 + h * 4 + x
        return pltpu.make_async_copy(b_part(d, 0), got.at[slot], b_recv.at[slot])

    def stays(d):
        return column(d)[1] == y

    def leaves(d):
        return column(d)[1] != y

    for d in (0, 1, 2, 6, 3, 7, 4, 5):
        if d == 0:
            keep.wait()
        else:
            a_arrival(d).wait_recv()
        for j in (2, 1, 3):
            b_copy(d, j).start()

        @pl.when(leaves(d))
        def _():
            b_copy(d, 0).start()

        @pl.when(stays(d))
        def _():
            b_keep(d).start()

    for i in range(1, 16):
        q_copy(i).wait_recv()
        total = total + sums[i - 1]
    sums_out[...] = total

    def take(s, _):
        ys, xs = lax.div(s, 8), lax.rem(s, 4)
        here = jnp.logical_and(ys == y, xs == x)

        @pl.when(jnp.logical_not(here))
        def _():
            remote(relay.at[0, :, pl.ds(0, WIDE)], got.at[s], b_send.at[0, 1], b_recv.at[s],
                   ys * 8 + zh * 4 + xs, los).wait_recv()

        @pl.when(here)
        def _():
            pltpu.make_async_copy(relay.at[0, :, pl.ds(0, WIDE)], got.at[s], b_recv.at[s]).wait()
        return 0

    lax.fori_loop(0, SEGS, take, 0)

    for copy in edges:
        copy.wait_send()
    for d in range(1, 8):
        a_copy(d).wait_send()
        p_copy(d).wait_send()
    for i in range(1, 16):
        q_copy(i).wait_send()
    for d in range(8):
        for j in (1, 2, 3):
            b_copy(d, j).wait_send()

        @pl.when(leaves(d))
        def _():
            b_copy(d, 0).wait_send()


def share(tau, right, left):
    vmem = pl.BlockSpec(memory_space=pltpu.VMEM)
    dma = pltpu.SemaphoreType.DMA
    return pl.pallas_call(
        share_kernel,
        out_shape=(jax.ShapeDtypeStruct((SEGS, 32, WIDE), F32), jax.ShapeDtypeStruct((8, 128), F32)),
        in_specs=[vmem] * 3,
        out_specs=(pl.BlockSpec(memory_space=pl.ANY), vmem),
        scratch_shapes=[
            pltpu.VMEM((ROWS, REACH), F32),
            pltpu.VMEM((ROWS, REACH), F32),
            pltpu.VMEM((ROWS, LENGTH), F32),
            pltpu.VMEM((8, 32, 1024), F32),
            pltpu.VMEM((8, 128), F32),
            pltpu.VMEM((7, 8, 128), F32),
            pltpu.VMEM((8, 128), F32),
            pltpu.VMEM((15, 8, 128), F32),
            dma((2,)),
            dma((2,)),
            dma((8,)),
            dma((8,)),
            dma((8, 4)),
            dma((SEGS,)),
            dma((7,)),
            dma((7,)),
            dma((15,)),
            dma((15,)),
        ],
        compiler_params=pltpu.CompilerParams(collective_id=0, has_side_effects=True, vmem_limit_bytes=24 << 20),
        name="share",
    )(tau, right, left)


def per_device(contrast, warmth, velocity, semi_extent, lookup):
    seg = lax.axis_index("seg")
    mine = lookup == seg
    own = jnp.sum(jnp.where(mine[:, None], semi_extent, 0).astype(F32), axis=0)
    h = lax.all_gather(own, "los", tiled=True)
    at = jnp.arange(ROWS)
    below = (h[None, :] < h[:, None]) | ((h[None, :] == h[:, None]) & (at[None, :] < at[:, None]))
    rank = jnp.sum(below.astype(jnp.int32), axis=1)
    hot = rank[:, None] == at[None, :]
    perm = jnp.sum(jnp.where(hot, at[:, None], 0), axis=0).astype(jnp.int32)
    reach = jnp.sum(jnp.where(hot, h[:, None], 0.0), axis=0).astype(jnp.int32)

    def by_lane(a):
        return a.reshape(ROWS, 128, 16).transpose(2, 0, 1)

    def in_order(a):
        return a.transpose(1, 2, 0).reshape(ROWS, -1)

    tau, edge = band_depth(perm, reach, by_lane(contrast), by_lane(warmth), by_lane(velocity))
    got, sums = share(in_order(tau), in_order(edge[:, :, :32]), in_order(edge[:, :, 96:]))
    scale = CELLS / jnp.sum(sums)
    return jnp.take(got, lookup, axis=0) * scale


def solution(mesh):
    return jax.shard_map(
        per_device,
        mesh=mesh,
        in_specs=(P("seg", None, "los"), P("seg", None, "los"), P("seg", None, "los"), P(None, "los"), P()),
        out_specs=P(None, "los", "seg"),
        check_vma=False,
    )
```

```python
import functools

import jax
import jax.numpy as jnp
from jax import lax
from jax.experimental import pallas as pl
from jax.experimental.pallas import tpu as pltpu
from jax.sharding import PartitionSpec as P

LOG2E = 1.4426950408889634
ROWS = 128
LENGTH = 2048
GROUPS = ROWS // 8
REACH = 512
SEGS, LOSS = 32, 4
WIDE = 256
CELLS = 33554432.0
MESH = pl.DeviceIdType.MESH
F32 = jnp.float32


def order_kernel(lookup, extent, order, tile, tiles, send, recv):
    seg, los = lax.axis_index("seg"), lax.axis_index("los")
    barrier = pltpu.get_barrier_semaphore()
    for j in range(1, LOSS):
        pl.semaphore_signal(barrier, inc=1, device_id=(seg, lax.rem(los + j, LOSS)), device_id_type=MESH)
    pl.semaphore_wait(barrier, LOSS - 1)
    row = jnp.int32(0)
    for i in range(SEGS):
        row = jnp.where(lookup[i] == seg, i, row)
    tile[...] = jnp.zeros((8, 128), F32)
    tile[0:1, 0:32] = extent[pl.ds(row, 1), :].astype(F32)
    copies = [
        pltpu.make_async_remote_copy(
            src_ref=tile, dst_ref=tiles.at[j - 1], send_sem=send.at[j - 1], recv_sem=recv.at[j - 1],
            device_id=(seg, lax.rem(los + j, LOSS)), device_id_type=MESH,
        )
        for j in range(1, LOSS)
    ]
    for copy in copies:
        copy.start()
    part = lax.broadcasted_iota(jnp.int32, (1, 128), 1) // 32
    for copy in copies:
        copy.wait_recv()
    h = jnp.zeros((1, 128), F32)
    for j in range(LOSS):
        values = (tile if j == 0 else tiles.at[j - 1])[0:1, :]
        owner = lax.rem(los + LOSS - j, LOSS)
        for l in range(LOSS):
            h = h + jnp.where(jnp.logical_and(part == l, owner == l), pltpu.roll(values, 32 * l, 1) if l else values, 0.0)
    i = lax.broadcasted_iota(jnp.int32, (128, 128), 0)
    j = lax.broadcasted_iota(jnp.int32, (128, 128), 1)
    across = jnp.broadcast_to(h, (128, 128))
    down = jnp.sum(jnp.where(i == j, across, 0.0), axis=1, keepdims=True)
    below = jnp.logical_or(across < down, jnp.logical_and(across == down, j < i))
    rank = jnp.sum(jnp.where(below, 1.0, 0.0), axis=1, keepdims=True)
    hot = rank == j.astype(F32)
    order[0:1, :] = jnp.sum(jnp.where(hot, i.astype(F32), 0.0), axis=0, keepdims=True).astype(jnp.int32)
    order[1:2, :] = jnp.sum(jnp.where(hot, down, 0.0), axis=0, keepdims=True).astype(jnp.int32)
    for copy in copies:
        copy.wait_send()


def sightline_order(lookup, extent):
    vmem = pl.BlockSpec(memory_space=pltpu.VMEM)
    return pl.pallas_call(
        order_kernel,
        out_shape=jax.ShapeDtypeStruct((2, ROWS), jnp.int32),
        in_specs=[pl.BlockSpec(memory_space=pltpu.SMEM), vmem],
        out_specs=vmem,
        scratch_shapes=[
            pltpu.VMEM((8, 128), F32),
            pltpu.VMEM((3, 8, 128), F32),
            pltpu.SemaphoreType.DMA((3,)),
            pltpu.SemaphoreType.DMA((3,)),
        ],
        compiler_params=pltpu.CompilerParams(collective_id=1, has_side_effects=True, vmem_limit_bytes=4 << 20),
        name="order",
    )(lookup, extent)


def band_kernel(table, d_ref, t_ref, v_ref, tau_ref, edge_ref, W, C, NB, N4, Q, M, Zb, S, E):
    lane = lax.broadcasted_iota(jnp.int32, (8, 128), 1)
    sub = lax.broadcasted_iota(jnp.int32, (8, 128), 0)
    zero = jnp.zeros((8, 128), F32)

    def gather(g, _):
        at = pl.ds(pl.multiple_of(g * 16, 16), 16)
        for i in range(8):
            y = table[0, g * 8 + i]
            W[at, i : i + 1, :] = d_ref[:, pl.ds(y, 1), :]
            NB[at, i : i + 1, :] = t_ref[:, pl.ds(y, 1), :]
            C[at, i : i + 1, :] = v_ref[:, pl.ds(y, 1), :]
        return 0

    lax.fori_loop(0, GROUPS, gather, 0)

    def prep(g, _):
        for t in range(16):
            a = g * 16 + t
            warmth = NB[a]
            contrast = W[a]
            nb = (-LOG2E / 169.0) / warmth
            C[a] = 0.5 * (C[a] + float(t))
            NB[a] = nb
            N4[a] = 4.0 * nb
            Q[a] = jnp.exp2(nb + nb)
            W[a] = ((0.3 / 13.0) * jnp.exp2(-1.2 * jnp.log2(warmth))) * (contrast * contrast)
            S[a] = zero
            E[a] = zero
        return 0

    lax.fori_loop(0, GROUPS, prep, 0)

    def group(g, _):
        hv = zero
        for i in range(8):
            hv = jnp.where(sub == i, table[1, g * 8 + i].astype(F32), hv)
        kout = lax.div(table[1, g * 8 + 7] + 15, 16)
        kin = lax.div(table[1, g * 8] - 15, 16)
        base = g * 16
        for r in range(16):
            Zb[1, r] = zero

        def place(dst, sk):
            shift = lax.rem(sk + 128, 128)
            inside = jnp.logical_and(lane >= sk, lane < sk + 128)
            for r in range(16):
                z = pltpu.roll(Zb[1 - dst, r], shift, 1)
                S[base + r] = S[base + r] + jnp.where(inside, z, 0.0)
                E[base + r] = E[base + r] + jnp.where(inside, 0.0, z)

        def cells(Z, kf, masked):
            for s in range(16):
                nb = NB[base + s]
                x = kf - C[base + s]
                m2 = N4[base + s] * x
                A = W[base + s] * jnp.exp2(m2 * x)
                R = jnp.exp2(m2 + nb)
                U = jnp.exp2(nb - m2)
                q = Q[base + s]

                def add(r, G):
                    term = G * M[r - s + 15] if masked else G
                    Z[r] = term if Z[r] is None else Z[r] + term

                add(8, A)
                G = H = A
                for i in range(1, 9):
                    H = H * U
                    add(8 - i, H)
                    if i < 8:
                        G = G * R
                        add(8 + i, G)
                    if i < 7:
                        R = R * q
                    if i < 8:
                        U = U * q

        def step(side, sk, before, dst):
            if side:
                hk = hv - (16 * side * sk).astype(F32)
                for i in range(31):
                    M[i] = jnp.where(hk >= float(side * (i - 15)), 1.0, 0.0)
            Z = [None] * 16
            place(dst, before)
            cells(Z, (8 * sk + 4).astype(F32), side)
            for r in range(16):
                Zb[dst, r] = Z[r]

        def edge_step(side, where, n, carry):
            before, dst = carry
            sk = where(n)
            step(side, sk, before, dst)
            return sk, 1 - dst

        def two_steps(n, carry):
            before, dst = carry
            one = jnp.where(2 * n < kin, 2 * n - kin, 2 * kin - 2 * n)
            two = jnp.where(2 * n + 1 < kin, 2 * n + 1 - kin, 2 * kin - 2 * n - 1)
            step(0, one, before, dst)
            step(0, two, one, 1 - dst)
            return two, dst

        carry = (jnp.int32(0), jnp.int32(0))
        carry = lax.fori_loop(0, kout - kin, functools.partial(edge_step, -1, lambda n: n - kout), carry)
        carry = lax.fori_loop(0, kout - kin, functools.partial(edge_step, 1, lambda n: kout - n), carry)
        carry = lax.fori_loop(0, kin, two_steps, carry)
        carry = edge_step(0, lambda n: jnp.int32(0), 0, carry)
        fin = 1 - carry[1]
        for r in range(16):
            S[base + r] = S[base + r] + Zb[fin, r]
        return 0

    lax.fori_loop(0, GROUPS, group, 0)

    def scatter(g, _):
        at = pl.ds(pl.multiple_of(g * 16, 16), 16)
        for i in range(8):
            y = table[0, g * 8 + i]
            tau_ref[:, pl.ds(y, 1), :] = S[at, i : i + 1, :]
            edge_ref[:, pl.ds(y, 1), :] = E[at, i : i + 1, :]
        return 0

    lax.fori_loop(0, GROUPS, scatter, 0)

def band_depth(order, d, t, v):
    whole = pl.BlockSpec((16, ROWS, 128), lambda i, *_: (0, 0, 0))
    table = pltpu.VMEM((GROUPS * 16, 8, 128), F32)
    return pl.pallas_call(
        band_kernel,
        out_shape=(jax.ShapeDtypeStruct((16, ROWS, 128), F32),) * 2,
        grid_spec=pltpu.PrefetchScalarGridSpec(
            num_scalar_prefetch=1, grid=(1,), in_specs=[whole] * 3, out_specs=[whole] * 2,
            scratch_shapes=[table] * 5 + [pltpu.VMEM((31, 8, 128), F32), pltpu.VMEM((2, 16, 8, 128), F32), table, table],
        ),
        compiler_params=pltpu.CompilerParams(vmem_limit_bytes=24 << 20),
        name="band",
    )(order, d, t, v)


def share_kernel(tau, right, left, got, sums_out, from_left, from_right, flux, relay, part, parts, local_sum, sums,
                 edge_send, edge_recv, a_send, a_recv, b_send, b_recv, p_send, p_recv, q_send, q_recv):
    seg, los = lax.axis_index("seg"), lax.axis_index("los")
    y, zh, x = lax.div(seg, 8), lax.rem(lax.div(seg, 4), 2), lax.rem(seg, 4)
    zl, core = lax.div(los, 2), lax.rem(los, 2)
    after, before = lax.rem(los + 1, LOSS), lax.rem(los + LOSS - 1, LOSS)
    me = zh * 4 + los

    def column(d):
        h = 1 - zh if d & 4 else zh
        l = (1 - zl if d & 2 else zl) * 2 + (1 - core if d & 1 else core)
        return h, l

    def plane(dy, dx):
        return lax.rem(y + dy, 4) * 8 + zh * 4 + lax.rem(x + dx, 4)

    barrier = pltpu.get_barrier_semaphore()

    def signal(s, l):
        pl.semaphore_signal(barrier, inc=1, device_id=(s, l), device_id_type=MESH)

    for d in range(1, 8):
        h, l = column(d)
        signal(y * 8 + h * 4 + x, l)
    for i in range(1, 16):
        signal(plane(i // 4, i % 4), los)
    pl.semaphore_wait(barrier, 22)

    def remote(src, dst, send, recv, s, l):
        return pltpu.make_async_remote_copy(
            src_ref=src, dst_ref=dst, send_sem=send, recv_sem=recv, device_id=(s, l), device_id_type=MESH
        )

    edges = [
        remote(right, from_left, edge_send.at[0], edge_recv.at[0], seg, after),
        remote(left, from_right, edge_send.at[1], edge_recv.at[1], seg, before),
    ]
    for copy in edges:
        copy.start()
    for copy in edges:
        copy.wait_recv()

    def rows_of(i, total):
        rows = pl.ds(pl.multiple_of(i * 8, 8), 8)
        for m in range(16):
            cols = pl.ds(m * 128, 128)
            depth = tau[rows, cols]
            if m < 4:
                depth = depth + from_left[rows, cols]
            if m >= 12:
                depth = depth + from_right[rows, pl.ds((m - 12) * 128, 128)]
            value = jnp.exp(-depth)
            flux[rows, cols] = value
            total = total + value
        return total

    part[...] = lax.fori_loop(0, GROUPS, rows_of, jnp.zeros((8, 128), F32))

    def a_part(d):
        h, l = column(d)
        return flux.at[pl.ds(pl.multiple_of(l * 32, 32), 32), pl.ds(pl.multiple_of(h * 1024, 1024), 1024)]

    def a_copy(d):
        h, l = column(d)
        return remote(a_part(d), relay.at[me], a_send.at[d], a_recv.at[me], y * 8 + h * 4 + x, l)

    def a_arrival(d):
        h, l = column(d)
        return remote(a_part(d), relay.at[h * 4 + l], a_send.at[d], a_recv.at[h * 4 + l], y * 8 + h * 4 + x, l)

    def p_copy(d):
        h, l = column(d)
        return remote(part, parts.at[d - 1], p_send.at[d - 1], p_recv.at[d - 1], y * 8 + h * 4 + x, l)

    for d in range(1, 8):
        p_copy(d).start()
    keep = pltpu.make_async_copy(a_part(0), relay.at[me], a_recv.at[me])
    for d in (4, 2, 6, 5, 3, 7, 1):
        a_copy(d).start()
    keep.start()

    total = part[...]
    for d in range(1, 8):
        p_copy(d).wait_recv()
        total = total + parts[d - 1]
    local_sum[...] = total

    def q_copy(i):
        return remote(local_sum, sums.at[i - 1], q_send.at[i - 1], q_recv.at[i - 1], plane(i // 4, i % 4), los)

    for i in range(1, 16):
        q_copy(i).start()

    def b_part(d, j):
        h, l = column(d)
        to = lax.rem(x + j, 4)
        return relay.at[h * 4 + l, :, pl.ds(pl.multiple_of(to * WIDE, WIDE), WIDE)]

    def b_copy(d, j):
        h, l = column(d)
        slot = y * 8 + h * 4 + x
        return remote(b_part(d, j), got.at[slot], b_send.at[d, j], b_recv.at[slot],
                      l * 8 + zh * 4 + lax.rem(x + j, 4), los)

    def b_keep(d):
        h, l = column(d)
        slot = y * 8 + h * 4 + x
        return pltpu.make_async_copy(b_part(d, 0), got.at[slot], b_recv.at[slot])

    def stays(d):
        return column(d)[1] == y

    def leaves(d):
        return column(d)[1] != y

    for d in (0, 1, 2, 6, 3, 7, 4, 5):
        if d == 0:
            keep.wait()
        else:
            a_arrival(d).wait_recv()
        for j in (2, 1, 3):
            b_copy(d, j).start()

        @pl.when(leaves(d))
        def _():
            b_copy(d, 0).start()

        @pl.when(stays(d))
        def _():
            b_keep(d).start()

    for i in range(1, 16):
        q_copy(i).wait_recv()
        total = total + sums[i - 1]
    sums_out[...] = total

    def take(s, _):
        ys, xs = lax.div(s, 8), lax.rem(s, 4)
        here = jnp.logical_and(ys == y, xs == x)

        @pl.when(jnp.logical_not(here))
        def _():
            remote(relay.at[0, :, pl.ds(0, WIDE)], got.at[s], b_send.at[0, 1], b_recv.at[s],
                   ys * 8 + zh * 4 + xs, los).wait_recv()

        @pl.when(here)
        def _():
            pltpu.make_async_copy(relay.at[0, :, pl.ds(0, WIDE)], got.at[s], b_recv.at[s]).wait()
        return 0

    lax.fori_loop(0, SEGS, take, 0)

    for copy in edges:
        copy.wait_send()
    for d in range(1, 8):
        a_copy(d).wait_send()
        p_copy(d).wait_send()
    for i in range(1, 16):
        q_copy(i).wait_send()
    for d in range(8):
        for j in (1, 2, 3):
            b_copy(d, j).wait_send()

        @pl.when(leaves(d))
        def _():
            b_copy(d, 0).wait_send()


def share(tau, right, left):
    vmem = pl.BlockSpec(memory_space=pltpu.VMEM)
    dma = pltpu.SemaphoreType.DMA
    return pl.pallas_call(
        share_kernel,
        out_shape=(jax.ShapeDtypeStruct((SEGS, 32, WIDE), F32), jax.ShapeDtypeStruct((8, 128), F32)),
        in_specs=[vmem] * 3,
        out_specs=(pl.BlockSpec(memory_space=pl.ANY), vmem),
        scratch_shapes=[
            pltpu.VMEM((ROWS, REACH), F32),
            pltpu.VMEM((ROWS, REACH), F32),
            pltpu.VMEM((ROWS, LENGTH), F32),
            pltpu.VMEM((8, 32, 1024), F32),
            pltpu.VMEM((8, 128), F32),
            pltpu.VMEM((7, 8, 128), F32),
            pltpu.VMEM((8, 128), F32),
            pltpu.VMEM((15, 8, 128), F32),
            dma((2,)),
            dma((2,)),
            dma((8,)),
            dma((8,)),
            dma((8, 4)),
            dma((SEGS,)),
            dma((7,)),
            dma((7,)),
            dma((15,)),
            dma((15,)),
        ],
        compiler_params=pltpu.CompilerParams(collective_id=0, has_side_effects=True, vmem_limit_bytes=10 << 20),
        name="share",
    )(tau, right, left)


def per_device(contrast, warmth, velocity, semi_extent, lookup):
    order = sightline_order(lookup, semi_extent)

    def by_lane(a):
        return a.reshape(ROWS, 128, 16).transpose(2, 0, 1)

    def in_order(a):
        return a.transpose(1, 2, 0).reshape(ROWS, -1)

    tau, edge = band_depth(order, by_lane(contrast), by_lane(warmth), by_lane(velocity))
    got, sums = share(in_order(tau), in_order(edge[:, :, :32]), in_order(edge[:, :, 96:]))
    scale = CELLS / jnp.sum(sums)
    return jnp.take(got, lookup, axis=0) * scale


def solution(mesh):
    return jax.shard_map(
        per_device,
        mesh=mesh,
        in_specs=(P("seg", None, "los"), P("seg", None, "los"), P("seg", None, "los"), P(None, "los"), P()),
        out_specs=P(None, "los", "seg"),
        check_vma=False,
    )
```

```python
import functools

import jax
import jax.numpy as jnp
from jax import lax
from jax.experimental import pallas as pl
from jax.experimental.pallas import tpu as pltpu
from jax.sharding import PartitionSpec as P

LOG2E = 1.4426950408889634
ROWS = 128
LENGTH = 2048
GROUPS = ROWS // 8
REACH = 512
SEGS, LOSS = 32, 4
WIDE = 256
CELLS = 33554432.0
MESH = pl.DeviceIdType.MESH
F32 = jnp.float32


def order_kernel(lookup, extent, d, t, v, order, d_out, t_out, v_out, fields, cells, tile, tiles, load, send, recv):
    loads = [pltpu.make_async_copy(ref, fields.at[n], load.at[n]) for n, ref in enumerate((d, t, v))]
    for copy in loads:
        copy.start()
    seg, los = lax.axis_index("seg"), lax.axis_index("los")
    barrier = pltpu.get_barrier_semaphore()
    for j in range(1, LOSS):
        pl.semaphore_signal(barrier, inc=1, device_id=(seg, lax.rem(los + j, LOSS)), device_id_type=MESH)
    pl.semaphore_wait(barrier, LOSS - 1)
    row = jnp.int32(0)
    for i in range(SEGS):
        row = jnp.where(lookup[i] == seg, i, row)
    tile[...] = jnp.zeros((8, 128), F32)
    tile[0:1, 0:32] = extent[pl.ds(row, 1), :].astype(F32)
    copies = [
        pltpu.make_async_remote_copy(
            src_ref=tile, dst_ref=tiles.at[j - 1], send_sem=send.at[j - 1], recv_sem=recv.at[j - 1],
            device_id=(seg, lax.rem(los + j, LOSS)), device_id_type=MESH,
        )
        for j in range(1, LOSS)
    ]
    for copy in copies:
        copy.start()
    for n, out in enumerate((d_out, t_out, v_out)):
        loads[n].wait()

        def columns(m, _):
            block = fields[n, :, pl.ds(pl.multiple_of(m * 128, 128), 128)].T
            cells[pl.ds(pl.multiple_of(m * 8, 8), 8)] = block.reshape(8, 16, 128)
            return 0

        lax.fori_loop(0, 16, columns, 0)
        for i in range(16):
            out[i] = cells[:, i, :].T
    part = lax.broadcasted_iota(jnp.int32, (1, 128), 1) // 32
    for copy in copies:
        copy.wait_recv()
    h = jnp.zeros((1, 128), F32)
    for j in range(LOSS):
        values = (tile if j == 0 else tiles.at[j - 1])[0:1, :]
        owner = lax.rem(los + LOSS - j, LOSS)
        for l in range(LOSS):
            h = h + jnp.where(jnp.logical_and(part == l, owner == l), pltpu.roll(values, 32 * l, 1) if l else values, 0.0)
    i = lax.broadcasted_iota(jnp.int32, (128, 128), 0)
    j = lax.broadcasted_iota(jnp.int32, (128, 128), 1)
    across = jnp.broadcast_to(h, (128, 128))
    down = jnp.sum(jnp.where(i == j, across, 0.0), axis=1, keepdims=True)
    below = jnp.logical_or(across < down, jnp.logical_and(across == down, j < i))
    rank = jnp.sum(jnp.where(below, 1.0, 0.0), axis=1, keepdims=True)
    hot = rank == j.astype(F32)
    order[0:1, :] = jnp.sum(jnp.where(hot, i.astype(F32), 0.0), axis=0, keepdims=True).astype(jnp.int32)
    order[1:2, :] = jnp.sum(jnp.where(hot, down, 0.0), axis=0, keepdims=True).astype(jnp.int32)
    for copy in copies:
        copy.wait_send()


def sightline_order(lookup, extent, d, t, v):
    vmem = pl.BlockSpec(memory_space=pltpu.VMEM)
    there = pl.BlockSpec(memory_space=pl.ANY)
    by_lane = jax.ShapeDtypeStruct((16, ROWS, 128), F32)
    return pl.pallas_call(
        order_kernel,
        out_shape=(jax.ShapeDtypeStruct((2, ROWS), jnp.int32), by_lane, by_lane, by_lane),
        in_specs=[pl.BlockSpec(memory_space=pltpu.SMEM), vmem, there, there, there],
        out_specs=(vmem,) * 4,
        scratch_shapes=[
            pltpu.VMEM((3, ROWS, LENGTH), F32),
            pltpu.VMEM((128, 16, 128), F32),
            pltpu.VMEM((8, 128), F32),
            pltpu.VMEM((3, 8, 128), F32),
            pltpu.SemaphoreType.DMA((3,)),
            pltpu.SemaphoreType.DMA((3,)),
            pltpu.SemaphoreType.DMA((3,)),
        ],
        compiler_params=pltpu.CompilerParams(collective_id=1, has_side_effects=True, vmem_limit_bytes=50 << 20),
        name="order",
    )(lookup, extent, d, t, v)


def band_kernel(table, d_ref, t_ref, v_ref, tau_ref, edge_ref, W, C, NB, N4, Q, M, Zb, S, E):
    lane = lax.broadcasted_iota(jnp.int32, (8, 128), 1)
    sub = lax.broadcasted_iota(jnp.int32, (8, 128), 0)
    zero = jnp.zeros((8, 128), F32)

    def gather(g, _):
        at = pl.ds(pl.multiple_of(g * 16, 16), 16)
        for i in range(8):
            y = table[0, g * 8 + i]
            W[at, i : i + 1, :] = d_ref[:, pl.ds(y, 1), :]
            NB[at, i : i + 1, :] = t_ref[:, pl.ds(y, 1), :]
            C[at, i : i + 1, :] = v_ref[:, pl.ds(y, 1), :]
        return 0

    lax.fori_loop(0, GROUPS, gather, 0)

    def prep(g, _):
        for t in range(16):
            a = g * 16 + t
            warmth = NB[a]
            contrast = W[a]
            nb = (-LOG2E / 169.0) / warmth
            C[a] = 0.5 * (C[a] + float(t))
            NB[a] = nb
            N4[a] = 4.0 * nb
            Q[a] = jnp.exp2(nb + nb)
            W[a] = ((0.3 / 13.0) * jnp.exp2(-1.2 * jnp.log2(warmth))) * (contrast * contrast)
            S[a] = zero
            E[a] = zero
        return 0

    lax.fori_loop(0, GROUPS, prep, 0)

    def group(g, _):
        hv = zero
        for i in range(8):
            hv = jnp.where(sub == i, table[1, g * 8 + i].astype(F32), hv)
        kout = lax.div(table[1, g * 8 + 7] + 15, 16)
        kin = lax.div(table[1, g * 8] - 15, 16)
        base = g * 16
        for r in range(16):
            Zb[1, r] = zero

        def place(dst, sk):
            shift = lax.rem(sk + 128, 128)
            inside = jnp.logical_and(lane >= sk, lane < sk + 128)
            for r in range(16):
                z = pltpu.roll(Zb[1 - dst, r], shift, 1)
                S[base + r] = S[base + r] + jnp.where(inside, z, 0.0)
                E[base + r] = E[base + r] + jnp.where(inside, 0.0, z)

        def cells(Z, kf, masked):
            for s in range(16):
                nb = NB[base + s]
                x = kf - C[base + s]
                m2 = N4[base + s] * x
                A = W[base + s] * jnp.exp2(m2 * x)
                R = jnp.exp2(m2 + nb)
                U = jnp.exp2(nb - m2)
                q = Q[base + s]

                def add(r, G):
                    term = G * M[r - s + 15] if masked else G
                    Z[r] = term if Z[r] is None else Z[r] + term

                add(8, A)
                G = H = A
                for i in range(1, 9):
                    H = H * U
                    add(8 - i, H)
                    if i < 8:
                        G = G * R
                        add(8 + i, G)
                    if i < 7:
                        R = R * q
                    if i < 8:
                        U = U * q

        def step(side, sk, before, dst):
            if side:
                hk = hv - (16 * side * sk).astype(F32)
                for i in range(31):
                    M[i] = jnp.where(hk >= float(side * (i - 15)), 1.0, 0.0)
            Z = [None] * 16
            place(dst, before)
            cells(Z, (8 * sk + 4).astype(F32), side)
            for r in range(16):
                Zb[dst, r] = Z[r]

        def edge_step(side, where, n, carry):
            before, dst = carry
            sk = where(n)
            step(side, sk, before, dst)
            return sk, 1 - dst

        def two_steps(n, carry):
            before, dst = carry
            one = jnp.where(2 * n < kin, 2 * n - kin, 2 * kin - 2 * n)
            two = jnp.where(2 * n + 1 < kin, 2 * n + 1 - kin, 2 * kin - 2 * n - 1)
            step(0, one, before, dst)
            step(0, two, one, 1 - dst)
            return two, dst

        carry = (jnp.int32(0), jnp.int32(0))
        carry = lax.fori_loop(0, kout - kin, functools.partial(edge_step, -1, lambda n: n - kout), carry)
        carry = lax.fori_loop(0, kout - kin, functools.partial(edge_step, 1, lambda n: kout - n), carry)
        carry = lax.fori_loop(0, kin, two_steps, carry)
        carry = lax.fori_loop(kin, kin + 1, functools.partial(edge_step, 0, lambda n: jnp.int32(0)), carry)
        fin = 1 - carry[1]
        for r in range(16):
            S[base + r] = S[base + r] + Zb[fin, r]
        return 0

    lax.fori_loop(0, GROUPS, group, 0)

    def scatter(g, _):
        at = pl.ds(pl.multiple_of(g * 16, 16), 16)
        for i in range(8):
            y = table[0, g * 8 + i]
            tau_ref[:, pl.ds(y, 1), :] = S[at, i : i + 1, :]
            edge_ref[:, pl.ds(y, 1), :] = E[at, i : i + 1, :]
        return 0

    lax.fori_loop(0, GROUPS, scatter, 0)

def band_depth(order, d, t, v):
    whole = pl.BlockSpec((16, ROWS, 128), lambda i, *_: (0, 0, 0))
    table = pltpu.VMEM((GROUPS * 16, 8, 128), F32)
    return pl.pallas_call(
        band_kernel,
        out_shape=(jax.ShapeDtypeStruct((16, ROWS, 128), F32),) * 2,
        grid_spec=pltpu.PrefetchScalarGridSpec(
            num_scalar_prefetch=1, grid=(1,), in_specs=[whole] * 3, out_specs=[whole] * 2,
            scratch_shapes=[table] * 5 + [pltpu.VMEM((31, 8, 128), F32), pltpu.VMEM((2, 16, 8, 128), F32), table, table],
        ),
        compiler_params=pltpu.CompilerParams(vmem_limit_bytes=24 << 20),
        name="band",
    )(order, d, t, v)


def share_kernel(tau, right, left, got, sums_out, from_left, from_right, flux, relay, part, parts, local_sum, sums,
                 edge_send, edge_recv, a_send, a_recv, b_send, b_recv, p_send, p_recv, q_send, q_recv):
    seg, los = lax.axis_index("seg"), lax.axis_index("los")
    y, zh, x = lax.div(seg, 8), lax.rem(lax.div(seg, 4), 2), lax.rem(seg, 4)
    zl, core = lax.div(los, 2), lax.rem(los, 2)
    after, before = lax.rem(los + 1, LOSS), lax.rem(los + LOSS - 1, LOSS)
    me = zh * 4 + los

    def column(d):
        h = 1 - zh if d & 4 else zh
        l = (1 - zl if d & 2 else zl) * 2 + (1 - core if d & 1 else core)
        return h, l

    def plane(dy, dx):
        return lax.rem(y + dy, 4) * 8 + zh * 4 + lax.rem(x + dx, 4)

    barrier = pltpu.get_barrier_semaphore()

    def signal(s, l):
        pl.semaphore_signal(barrier, inc=1, device_id=(s, l), device_id_type=MESH)

    for d in range(1, 8):
        h, l = column(d)
        signal(y * 8 + h * 4 + x, l)
    for i in range(1, 16):
        signal(plane(i // 4, i % 4), los)
    pl.semaphore_wait(barrier, 22)

    def remote(src, dst, send, recv, s, l):
        return pltpu.make_async_remote_copy(
            src_ref=src, dst_ref=dst, send_sem=send, recv_sem=recv, device_id=(s, l), device_id_type=MESH
        )

    edges = [
        remote(right, from_left, edge_send.at[0], edge_recv.at[0], seg, after),
        remote(left, from_right, edge_send.at[1], edge_recv.at[1], seg, before),
    ]
    for copy in edges:
        copy.start()
    for copy in edges:
        copy.wait_recv()

    def rows_of(i, total):
        rows = pl.ds(pl.multiple_of(i * 8, 8), 8)
        for m in range(16):
            cols = pl.ds(m * 128, 128)
            depth = tau[rows, cols]
            if m < 4:
                depth = depth + from_left[rows, cols]
            if m >= 12:
                depth = depth + from_right[rows, pl.ds((m - 12) * 128, 128)]
            value = jnp.exp(-depth)
            flux[rows, cols] = value
            total = total + value
        return total

    part[...] = lax.fori_loop(0, GROUPS, rows_of, jnp.zeros((8, 128), F32))

    def a_part(d):
        h, l = column(d)
        return flux.at[pl.ds(pl.multiple_of(l * 32, 32), 32), pl.ds(pl.multiple_of(h * 1024, 1024), 1024)]

    def a_copy(d):
        h, l = column(d)
        return remote(a_part(d), relay.at[me], a_send.at[d], a_recv.at[me], y * 8 + h * 4 + x, l)

    def a_arrival(d):
        h, l = column(d)
        return remote(a_part(d), relay.at[h * 4 + l], a_send.at[d], a_recv.at[h * 4 + l], y * 8 + h * 4 + x, l)

    def p_copy(d):
        h, l = column(d)
        return remote(part, parts.at[d - 1], p_send.at[d - 1], p_recv.at[d - 1], y * 8 + h * 4 + x, l)

    for d in range(1, 8):
        p_copy(d).start()
    keep = pltpu.make_async_copy(a_part(0), relay.at[me], a_recv.at[me])
    for d in (4, 2, 6, 5, 3, 7, 1):
        a_copy(d).start()
    keep.start()

    total = part[...]
    for d in range(1, 8):
        p_copy(d).wait_recv()
        total = total + parts[d - 1]
    local_sum[...] = total

    def q_copy(i):
        return remote(local_sum, sums.at[i - 1], q_send.at[i - 1], q_recv.at[i - 1], plane(i // 4, i % 4), los)

    for i in range(1, 16):
        q_copy(i).start()

    def b_part(d, j):
        h, l = column(d)
        to = lax.rem(x + j, 4)
        return relay.at[h * 4 + l, :, pl.ds(pl.multiple_of(to * WIDE, WIDE), WIDE)]

    def b_copy(d, j):
        h, l = column(d)
        slot = y * 8 + h * 4 + x
        return remote(b_part(d, j), got.at[slot], b_send.at[d, j], b_recv.at[slot],
                      l * 8 + zh * 4 + lax.rem(x + j, 4), los)

    def b_keep(d):
        h, l = column(d)
        slot = y * 8 + h * 4 + x
        return pltpu.make_async_copy(b_part(d, 0), got.at[slot], b_recv.at[slot])

    def stays(d):
        return column(d)[1] == y

    def leaves(d):
        return column(d)[1] != y

    for d in (0, 1, 2, 6, 3, 7, 4, 5):
        if d == 0:
            keep.wait()
        else:
            a_arrival(d).wait_recv()
        for j in (2, 1, 3):
            b_copy(d, j).start()

        @pl.when(leaves(d))
        def _():
            b_copy(d, 0).start()

        @pl.when(stays(d))
        def _():
            b_keep(d).start()

    for i in range(1, 16):
        q_copy(i).wait_recv()
        total = total + sums[i - 1]
    sums_out[...] = total

    def take(s, _):
        ys, xs = lax.div(s, 8), lax.rem(s, 4)
        here = jnp.logical_and(ys == y, xs == x)

        @pl.when(jnp.logical_not(here))
        def _():
            remote(relay.at[0, :, pl.ds(0, WIDE)], got.at[s], b_send.at[0, 1], b_recv.at[s],
                   ys * 8 + zh * 4 + xs, los).wait_recv()

        @pl.when(here)
        def _():
            pltpu.make_async_copy(relay.at[0, :, pl.ds(0, WIDE)], got.at[s], b_recv.at[s]).wait()
        return 0

    lax.fori_loop(0, SEGS, take, 0)

    for copy in edges:
        copy.wait_send()
    for d in range(1, 8):
        a_copy(d).wait_send()
        p_copy(d).wait_send()
    for i in range(1, 16):
        q_copy(i).wait_send()
    for d in range(8):
        for j in (1, 2, 3):
            b_copy(d, j).wait_send()

        @pl.when(leaves(d))
        def _():
            b_copy(d, 0).wait_send()


def share(tau, right, left):
    vmem = pl.BlockSpec(memory_space=pltpu.VMEM)
    dma = pltpu.SemaphoreType.DMA
    return pl.pallas_call(
        share_kernel,
        out_shape=(jax.ShapeDtypeStruct((SEGS, 32, WIDE), F32), jax.ShapeDtypeStruct((8, 128), F32)),
        in_specs=[vmem] * 3,
        out_specs=(pl.BlockSpec(memory_space=pl.ANY), vmem),
        scratch_shapes=[
            pltpu.VMEM((ROWS, REACH), F32),
            pltpu.VMEM((ROWS, REACH), F32),
            pltpu.VMEM((ROWS, LENGTH), F32),
            pltpu.VMEM((8, 32, 1024), F32),
            pltpu.VMEM((8, 128), F32),
            pltpu.VMEM((7, 8, 128), F32),
            pltpu.VMEM((8, 128), F32),
            pltpu.VMEM((15, 8, 128), F32),
            dma((2,)),
            dma((2,)),
            dma((8,)),
            dma((8,)),
            dma((8, 4)),
            dma((SEGS,)),
            dma((7,)),
            dma((7,)),
            dma((15,)),
            dma((15,)),
        ],
        compiler_params=pltpu.CompilerParams(collective_id=0, has_side_effects=True, vmem_limit_bytes=10 << 20),
        name="share",
    )(tau, right, left)


def per_device(contrast, warmth, velocity, semi_extent, lookup):
    shape = (ROWS, LENGTH)
    order, d, t, v = sightline_order(
        lookup, semi_extent, contrast.reshape(shape), warmth.reshape(shape), velocity.reshape(shape)
    )

    def in_order(a):
        return a.transpose(1, 2, 0).reshape(ROWS, -1)

    tau, edge = band_depth(order, d, t, v)
    got, sums = share(in_order(tau), in_order(edge[:, :, :32]), in_order(edge[:, :, 96:]))
    scale = CELLS / jnp.sum(sums)
    return jnp.take(got, lookup, axis=0) * scale


def solution(mesh):
    return jax.shard_map(
        per_device,
        mesh=mesh,
        in_specs=(P("seg", None, "los"), P("seg", None, "los"), P("seg", None, "los"), P(None, "los"), P()),
        out_specs=P(None, "los", "seg"),
        check_vma=False,
    )
```

```python
import functools

import jax
import jax.numpy as jnp
from jax import lax
from jax.experimental import pallas as pl
from jax.experimental.pallas import tpu as pltpu
from jax.sharding import PartitionSpec as P

LOG2E = 1.4426950408889634
ROWS = 128
LENGTH = 2048
GROUPS = ROWS // 8
REACH = 512
SEGS, LOSS = 32, 4
WIDE = 256
CELLS = 33554432.0
MESH = pl.DeviceIdType.MESH
F32 = jnp.float32


def order_kernel(lookup, extent, d, t, v, order, d_out, t_out, v_out, fields, cells, tile, tiles, load, send, recv):
    loads = [pltpu.make_async_copy(ref, fields.at[n], load.at[n]) for n, ref in enumerate((d, t, v))]
    for copy in loads:
        copy.start()
    seg, los = lax.axis_index("seg"), lax.axis_index("los")
    barrier = pltpu.get_barrier_semaphore()
    for j in range(1, LOSS):
        pl.semaphore_signal(barrier, inc=1, device_id=(seg, lax.rem(los + j, LOSS)), device_id_type=MESH)

    def turn(n):
        loads[n].wait()

        def columns(m, _):
            block = fields[n, :, pl.ds(pl.multiple_of(m * 128, 128), 128)].T
            cells[pl.ds(pl.multiple_of(m * 8, 8), 8)] = block.reshape(8, 16, 128)
            return 0

        lax.fori_loop(0, 16, columns, 0)
        for i in range(16):
            (d_out, t_out, v_out)[n][i] = cells[:, i, :].T

    turn(0)
    pl.semaphore_wait(barrier, LOSS - 1)
    row = jnp.int32(0)
    for i in range(SEGS):
        row = jnp.where(lookup[i] == seg, i, row)
    tile[...] = jnp.zeros((8, 128), F32)
    tile[0:1, 0:32] = extent[pl.ds(row, 1), :].astype(F32)
    copies = [
        pltpu.make_async_remote_copy(
            src_ref=tile, dst_ref=tiles.at[j - 1], send_sem=send.at[j - 1], recv_sem=recv.at[j - 1],
            device_id=(seg, lax.rem(los + j, LOSS)), device_id_type=MESH,
        )
        for j in range(1, LOSS)
    ]
    for copy in copies:
        copy.start()
    turn(1)
    turn(2)
    part = lax.broadcasted_iota(jnp.int32, (1, 128), 1) // 32
    for copy in copies:
        copy.wait_recv()
    h = jnp.zeros((1, 128), F32)
    for j in range(LOSS):
        values = (tile if j == 0 else tiles.at[j - 1])[0:1, :]
        owner = lax.rem(los + LOSS - j, LOSS)
        for l in range(LOSS):
            h = h + jnp.where(jnp.logical_and(part == l, owner == l), pltpu.roll(values, 32 * l, 1) if l else values, 0.0)
    i = lax.broadcasted_iota(jnp.int32, (128, 128), 0)
    j = lax.broadcasted_iota(jnp.int32, (128, 128), 1)
    across = jnp.broadcast_to(h, (128, 128))
    down = jnp.sum(jnp.where(i == j, across, 0.0), axis=1, keepdims=True)
    below = jnp.logical_or(across < down, jnp.logical_and(across == down, j < i))
    rank = jnp.sum(jnp.where(below, 1.0, 0.0), axis=1, keepdims=True)
    hot = rank == j.astype(F32)
    order[0:1, :] = jnp.sum(jnp.where(hot, i.astype(F32), 0.0), axis=0, keepdims=True).astype(jnp.int32)
    order[1:2, :] = jnp.sum(jnp.where(hot, down, 0.0), axis=0, keepdims=True).astype(jnp.int32)
    for copy in copies:
        copy.wait_send()


def sightline_order(lookup, extent, d, t, v):
    vmem = pl.BlockSpec(memory_space=pltpu.VMEM)
    there = pl.BlockSpec(memory_space=pl.ANY)
    by_lane = jax.ShapeDtypeStruct((16, ROWS, 128), F32)
    return pl.pallas_call(
        order_kernel,
        out_shape=(jax.ShapeDtypeStruct((2, ROWS), jnp.int32), by_lane, by_lane, by_lane),
        in_specs=[pl.BlockSpec(memory_space=pltpu.SMEM), vmem, there, there, there],
        out_specs=(vmem,) * 4,
        scratch_shapes=[
            pltpu.VMEM((3, ROWS, LENGTH), F32),
            pltpu.VMEM((128, 16, 128), F32),
            pltpu.VMEM((8, 128), F32),
            pltpu.VMEM((3, 8, 128), F32),
            pltpu.SemaphoreType.DMA((3,)),
            pltpu.SemaphoreType.DMA((3,)),
            pltpu.SemaphoreType.DMA((3,)),
        ],
        compiler_params=pltpu.CompilerParams(collective_id=1, has_side_effects=True, vmem_limit_bytes=50 << 20),
        name="order",
    )(lookup, extent, d, t, v)


def band_kernel(table, d_ref, t_ref, v_ref, tau_ref, edge_ref, W, C, NB, N4, Q, M, Zb, S, E):
    lane = lax.broadcasted_iota(jnp.int32, (8, 128), 1)
    sub = lax.broadcasted_iota(jnp.int32, (8, 128), 0)
    zero = jnp.zeros((8, 128), F32)

    def gather(g, _):
        at = pl.ds(pl.multiple_of(g * 16, 16), 16)
        for i in range(8):
            y = table[0, g * 8 + i]
            W[at, i : i + 1, :] = d_ref[:, pl.ds(y, 1), :]
            NB[at, i : i + 1, :] = t_ref[:, pl.ds(y, 1), :]
            C[at, i : i + 1, :] = v_ref[:, pl.ds(y, 1), :]
        return 0

    lax.fori_loop(0, GROUPS, gather, 0)

    def prep(g, _):
        for t in range(16):
            a = g * 16 + t
            warmth = NB[a]
            contrast = W[a]
            nb = (-LOG2E / 169.0) / warmth
            C[a] = 0.5 * (C[a] + float(t))
            NB[a] = nb
            N4[a] = 4.0 * nb
            Q[a] = jnp.exp2(nb + nb)
            W[a] = ((0.3 / 13.0) * jnp.exp2(-1.2 * jnp.log2(warmth))) * (contrast * contrast)
            S[a] = zero
            E[a] = zero
        return 0

    lax.fori_loop(0, GROUPS, prep, 0)

    def group(g, _):
        hv = zero
        for i in range(8):
            hv = jnp.where(sub == i, table[1, g * 8 + i].astype(F32), hv)
        kout = lax.div(table[1, g * 8 + 7] + 15, 16)
        kin = lax.div(table[1, g * 8] - 15, 16)
        base = g * 16
        for r in range(16):
            Zb[1, r] = zero

        def place(dst, sk):
            shift = lax.rem(sk + 128, 128)
            inside = jnp.logical_and(lane >= sk, lane < sk + 128)
            for r in range(16):
                z = pltpu.roll(Zb[1 - dst, r], shift, 1)
                S[base + r] = S[base + r] + jnp.where(inside, z, 0.0)
                E[base + r] = E[base + r] + jnp.where(inside, 0.0, z)

        def cells(Z, kf, masked):
            for s in range(16):
                nb = NB[base + s]
                x = kf - C[base + s]
                m2 = N4[base + s] * x
                A = W[base + s] * jnp.exp2(m2 * x)
                R = jnp.exp2(m2 + nb)
                U = jnp.exp2(nb - m2)
                q = Q[base + s]

                def add(r, G):
                    term = G * M[r - s + 15] if masked else G
                    Z[r] = term if Z[r] is None else Z[r] + term

                add(8, A)
                G = H = A
                for i in range(1, 9):
                    H = H * U
                    add(8 - i, H)
                    if i < 8:
                        G = G * R
                        add(8 + i, G)
                    if i < 7:
                        R = R * q
                    if i < 8:
                        U = U * q

        def step(side, sk, before, dst):
            if side:
                hk = hv - (16 * side * sk).astype(F32)
                for i in range(31):
                    M[i] = jnp.where(hk >= float(side * (i - 15)), 1.0, 0.0)
            Z = [None] * 16
            place(dst, before)
            cells(Z, (8 * sk + 4).astype(F32), side)
            for r in range(16):
                Zb[dst, r] = Z[r]

        def edge_step(side, where, n, carry):
            before, dst = carry
            sk = where(n)
            step(side, sk, before, dst)
            return sk, 1 - dst

        def two_steps(n, carry):
            before, dst = carry
            one = jnp.where(2 * n < kin, 2 * n - kin, 2 * kin - 2 * n)
            two = jnp.where(2 * n + 1 < kin, 2 * n + 1 - kin, 2 * kin - 2 * n - 1)
            step(0, one, before, dst)
            step(0, two, one, 1 - dst)
            return two, dst

        carry = (jnp.int32(0), jnp.int32(0))
        carry = lax.fori_loop(0, kout - kin, functools.partial(edge_step, -1, lambda n: n - kout), carry)
        carry = lax.fori_loop(0, kout - kin, functools.partial(edge_step, 1, lambda n: kout - n), carry)
        carry = lax.fori_loop(0, kin, two_steps, carry)
        carry = lax.fori_loop(kin, kin + 1, functools.partial(edge_step, 0, lambda n: jnp.int32(0)), carry)
        fin = 1 - carry[1]
        for r in range(16):
            S[base + r] = S[base + r] + Zb[fin, r]
        return 0

    lax.fori_loop(0, GROUPS, group, 0)

    def scatter(g, _):
        at = pl.ds(pl.multiple_of(g * 16, 16), 16)
        for i in range(8):
            y = table[0, g * 8 + i]
            tau_ref[:, pl.ds(y, 1), :] = S[at, i : i + 1, :]
            edge_ref[:, pl.ds(y, 1), :] = E[at, i : i + 1, :]
        return 0

    lax.fori_loop(0, GROUPS, scatter, 0)

def band_depth(order, d, t, v):
    whole = pl.BlockSpec((16, ROWS, 128), lambda i, *_: (0, 0, 0))
    table = pltpu.VMEM((GROUPS * 16, 8, 128), F32)
    return pl.pallas_call(
        band_kernel,
        out_shape=(jax.ShapeDtypeStruct((16, ROWS, 128), F32),) * 2,
        grid_spec=pltpu.PrefetchScalarGridSpec(
            num_scalar_prefetch=1, grid=(1,), in_specs=[whole] * 3, out_specs=[whole] * 2,
            scratch_shapes=[table] * 5 + [pltpu.VMEM((31, 8, 128), F32), pltpu.VMEM((2, 16, 8, 128), F32), table, table],
        ),
        compiler_params=pltpu.CompilerParams(vmem_limit_bytes=24 << 20),
        name="band",
    )(order, d, t, v)


def share_kernel(tau, edge, got, sums_out, right, left, from_left, from_right, cells, flux, relay, part, parts, local_sum, sums,
                 edge_send, edge_recv, a_send, a_recv, b_send, b_recv, p_send, p_recv, q_send, q_recv):
    seg, los = lax.axis_index("seg"), lax.axis_index("los")
    y, zh, x = lax.div(seg, 8), lax.rem(lax.div(seg, 4), 2), lax.rem(seg, 4)
    zl, core = lax.div(los, 2), lax.rem(los, 2)
    after, before = lax.rem(los + 1, LOSS), lax.rem(los + LOSS - 1, LOSS)
    me = zh * 4 + los

    def column(d):
        h = 1 - zh if d & 4 else zh
        l = (1 - zl if d & 2 else zl) * 2 + (1 - core if d & 1 else core)
        return h, l

    def plane(dy, dx):
        return lax.rem(y + dy, 4) * 8 + zh * 4 + lax.rem(x + dx, 4)

    barrier = pltpu.get_barrier_semaphore()

    def signal(s, l):
        pl.semaphore_signal(barrier, inc=1, device_id=(s, l), device_id_type=MESH)

    for d in range(1, 8):
        h, l = column(d)
        signal(y * 8 + h * 4 + x, l)
    for i in range(1, 16):
        signal(plane(i // 4, i % 4), los)
    for i in range(16):
        block = edge[i].T
        right[:, i, :] = block[0:32]
        left[:, i, :] = block[96:128]
    pl.semaphore_wait(barrier, 22)

    def remote(src, dst, send, recv, s, l):
        return pltpu.make_async_remote_copy(
            src_ref=src, dst_ref=dst, send_sem=send, recv_sem=recv, device_id=(s, l), device_id_type=MESH
        )

    edges = [
        remote(right, from_left, edge_send.at[0], edge_recv.at[0], seg, after),
        remote(left, from_right, edge_send.at[1], edge_recv.at[1], seg, before),
    ]
    for copy in edges:
        copy.start()
    for i in range(16):
        cells[:, i, :] = tau[i].T

    def depth_of(m):
        return cells[m * 8 : m * 8 + 8].reshape(128, 128)

    def take_flux(m, depth):
        value = jnp.exp(-depth)
        flux[:, m * 128 : (m + 1) * 128] = value.T
        return jnp.sum(value.reshape(16, 8, 128), axis=0)

    total = jnp.zeros((8, 128), F32)
    for m in range(4, 12):
        total = total + take_flux(m, depth_of(m))
    for copy in edges:
        copy.wait_recv()
    for m in range(4):
        total = total + take_flux(m, depth_of(m) + from_left[m * 8 : m * 8 + 8].reshape(128, 128))
        total = total + take_flux(m + 12, depth_of(m + 12) + from_right[m * 8 : m * 8 + 8].reshape(128, 128))
    part[...] = total

    def a_part(d):
        h, l = column(d)
        return flux.at[pl.ds(pl.multiple_of(l * 32, 32), 32), pl.ds(pl.multiple_of(h * 1024, 1024), 1024)]

    def a_copy(d):
        h, l = column(d)
        return remote(a_part(d), relay.at[me], a_send.at[d], a_recv.at[me], y * 8 + h * 4 + x, l)

    def a_arrival(d):
        h, l = column(d)
        return remote(a_part(d), relay.at[h * 4 + l], a_send.at[d], a_recv.at[h * 4 + l], y * 8 + h * 4 + x, l)

    def p_copy(d):
        h, l = column(d)
        return remote(part, parts.at[d - 1], p_send.at[d - 1], p_recv.at[d - 1], y * 8 + h * 4 + x, l)

    for d in range(1, 8):
        p_copy(d).start()
    keep = pltpu.make_async_copy(a_part(0), relay.at[me], a_recv.at[me])
    for d in (4, 2, 6, 5, 3, 7, 1):
        a_copy(d).start()
    keep.start()

    total = part[...]
    for d in range(1, 8):
        p_copy(d).wait_recv()
        total = total + parts[d - 1]
    local_sum[...] = total

    def q_copy(i):
        return remote(local_sum, sums.at[i - 1], q_send.at[i - 1], q_recv.at[i - 1], plane(i // 4, i % 4), los)

    for i in range(1, 16):
        q_copy(i).start()

    def b_part(d, j):
        h, l = column(d)
        to = lax.rem(x + j, 4)
        return relay.at[h * 4 + l, :, pl.ds(pl.multiple_of(to * WIDE, WIDE), WIDE)]

    def b_copy(d, j):
        h, l = column(d)
        slot = y * 8 + h * 4 + x
        return remote(b_part(d, j), got.at[slot], b_send.at[d, j], b_recv.at[slot],
                      l * 8 + zh * 4 + lax.rem(x + j, 4), los)

    def b_keep(d):
        h, l = column(d)
        slot = y * 8 + h * 4 + x
        return pltpu.make_async_copy(b_part(d, 0), got.at[slot], b_recv.at[slot])

    def stays(d):
        return column(d)[1] == y

    def leaves(d):
        return column(d)[1] != y

    for d in (0, 1, 2, 6, 3, 7, 4, 5):
        if d == 0:
            keep.wait()
        else:
            a_arrival(d).wait_recv()
        for j in (2, 1, 3):
            b_copy(d, j).start()

        @pl.when(leaves(d))
        def _():
            b_copy(d, 0).start()

        @pl.when(stays(d))
        def _():
            b_keep(d).start()

    for i in range(1, 16):
        q_copy(i).wait_recv()
        total = total + sums[i - 1]
    sums_out[...] = total

    def take(s, _):
        ys, xs = lax.div(s, 8), lax.rem(s, 4)
        here = jnp.logical_and(ys == y, xs == x)

        @pl.when(jnp.logical_not(here))
        def _():
            remote(relay.at[0, :, pl.ds(0, WIDE)], got.at[s], b_send.at[0, 1], b_recv.at[s],
                   ys * 8 + zh * 4 + xs, los).wait_recv()

        @pl.when(here)
        def _():
            pltpu.make_async_copy(relay.at[0, :, pl.ds(0, WIDE)], got.at[s], b_recv.at[s]).wait()
        return 0

    lax.fori_loop(0, SEGS, take, 0)

    for copy in edges:
        copy.wait_send()
    for d in range(1, 8):
        a_copy(d).wait_send()
        p_copy(d).wait_send()
    for i in range(1, 16):
        q_copy(i).wait_send()
    for d in range(8):
        for j in (1, 2, 3):
            b_copy(d, j).wait_send()

        @pl.when(leaves(d))
        def _():
            b_copy(d, 0).wait_send()


def share(tau, edge):
    vmem = pl.BlockSpec(memory_space=pltpu.VMEM)
    dma = pltpu.SemaphoreType.DMA
    side = pltpu.VMEM((REACH // 16, 16, ROWS), F32)
    return pl.pallas_call(
        share_kernel,
        out_shape=(jax.ShapeDtypeStruct((SEGS, 32, WIDE), F32), jax.ShapeDtypeStruct((8, 128), F32)),
        in_specs=[vmem] * 2,
        out_specs=(pl.BlockSpec(memory_space=pl.ANY), vmem),
        scratch_shapes=[
            side,
            side,
            side,
            side,
            pltpu.VMEM((128, 16, ROWS), F32),
            pltpu.VMEM((ROWS, LENGTH), F32),
            pltpu.VMEM((8, 32, 1024), F32),
            pltpu.VMEM((8, 128), F32),
            pltpu.VMEM((7, 8, 128), F32),
            pltpu.VMEM((8, 128), F32),
            pltpu.VMEM((15, 8, 128), F32),
            dma((2,)),
            dma((2,)),
            dma((8,)),
            dma((8,)),
            dma((8, 4)),
            dma((SEGS,)),
            dma((7,)),
            dma((7,)),
            dma((15,)),
            dma((15,)),
        ],
        compiler_params=pltpu.CompilerParams(collective_id=0, has_side_effects=True, vmem_limit_bytes=12 << 20),
        name="share",
    )(tau, edge)


def finish_kernel(lookup, got, sums, flux):
    scale = CELLS / jnp.sum(sums[...], axis=(0, 1), keepdims=True)

    def row(k, _):
        flux[k] = got[lookup[k]] * scale
        return 0

    lax.fori_loop(0, SEGS, row, 0)


def finish(lookup, got, sums):
    vmem = pl.BlockSpec(memory_space=pltpu.VMEM)
    return pl.pallas_call(
        finish_kernel,
        out_shape=jax.ShapeDtypeStruct((SEGS, 32, WIDE), F32),
        in_specs=[pl.BlockSpec(memory_space=pltpu.SMEM), vmem, vmem],
        out_specs=vmem,
        compiler_params=pltpu.CompilerParams(vmem_limit_bytes=8 << 20),
        name="finish",
    )(lookup, got, sums)


def per_device(contrast, warmth, velocity, semi_extent, lookup):
    shape = (ROWS, LENGTH)
    order, d, t, v = sightline_order(
        lookup, semi_extent, contrast.reshape(shape), warmth.reshape(shape), velocity.reshape(shape)
    )

    tau, edge = band_depth(order, d, t, v)
    got, sums = share(tau, edge)
    return finish(lookup, got, sums)


def solution(mesh):
    return jax.shard_map(
        per_device,
        mesh=mesh,
        in_specs=(P("seg", None, "los"), P("seg", None, "los"), P("seg", None, "los"), P(None, "los"), P()),
        out_specs=P(None, "los", "seg"),
        check_vma=False,
    )
```

```python
import functools

import jax
import jax.numpy as jnp
from jax import lax
from jax.experimental import pallas as pl
from jax.experimental.pallas import tpu as pltpu
from jax.sharding import PartitionSpec as P

LOG2E = 1.4426950408889634
ROWS = 128
LENGTH = 2048
GROUPS = ROWS // 8
REACH = 512
SEGS, LOSS = 32, 4
WIDE = 256
CELLS = 33554432.0
MESH = pl.DeviceIdType.MESH
F32 = jnp.float32


def order_kernel(lookup, extent, d, t, v, order, d_out, t_out, v_out, fields, cells, tile, tiles, load, send, recv):
    loads = [pltpu.make_async_copy(ref, fields.at[n], load.at[n]) for n, ref in enumerate((d, t, v))]
    for copy in loads:
        copy.start()
    seg, los = lax.axis_index("seg"), lax.axis_index("los")
    barrier = pltpu.get_barrier_semaphore()
    for j in range(1, LOSS):
        pl.semaphore_signal(barrier, inc=1, device_id=(seg, lax.rem(los + j, LOSS)), device_id_type=MESH)

    def turn(n):
        loads[n].wait()

        for m in range(16):
            cells[m * 128 : (m + 1) * 128] = fields[n, :, m * 128 : (m + 1) * 128].T
        for i in range(16):
            (d_out, t_out, v_out)[n][i] = cells[pl.ds(i, 128, stride=16), :].T

    turn(0)
    pl.semaphore_wait(barrier, LOSS - 1)
    row = jnp.int32(0)
    for i in range(SEGS):
        row = jnp.where(lookup[i] == seg, i, row)
    tile[...] = jnp.zeros((8, 128), F32)
    tile[0:1, 0:32] = extent[pl.ds(row, 1), :].astype(F32)
    copies = [
        pltpu.make_async_remote_copy(
            src_ref=tile, dst_ref=tiles.at[j - 1], send_sem=send.at[j - 1], recv_sem=recv.at[j - 1],
            device_id=(seg, lax.rem(los + j, LOSS)), device_id_type=MESH,
        )
        for j in range(1, LOSS)
    ]
    for copy in copies:
        copy.start()
    turn(1)
    turn(2)
    part = lax.broadcasted_iota(jnp.int32, (1, 128), 1) // 32
    for copy in copies:
        copy.wait_recv()
    h = jnp.zeros((1, 128), F32)
    for j in range(LOSS):
        values = (tile if j == 0 else tiles.at[j - 1])[0:1, :]
        owner = lax.rem(los + LOSS - j, LOSS)
        for l in range(LOSS):
            h = h + jnp.where(jnp.logical_and(part == l, owner == l), pltpu.roll(values, 32 * l, 1) if l else values, 0.0)
    i = lax.broadcasted_iota(jnp.int32, (128, 128), 0)
    j = lax.broadcasted_iota(jnp.int32, (128, 128), 1)
    across = jnp.broadcast_to(h, (128, 128))
    down = jnp.sum(jnp.where(i == j, across, 0.0), axis=1, keepdims=True)
    below = jnp.logical_or(across < down, jnp.logical_and(across == down, j < i))
    rank = jnp.sum(jnp.where(below, 1.0, 0.0), axis=1, keepdims=True)
    hot = rank == j.astype(F32)
    order[0:1, :] = jnp.sum(jnp.where(hot, i.astype(F32), 0.0), axis=0, keepdims=True).astype(jnp.int32)
    order[1:2, :] = jnp.sum(jnp.where(hot, down, 0.0), axis=0, keepdims=True).astype(jnp.int32)
    for copy in copies:
        copy.wait_send()


def sightline_order(lookup, extent, d, t, v):
    vmem = pl.BlockSpec(memory_space=pltpu.VMEM)
    there = pl.BlockSpec(memory_space=pl.ANY)
    by_lane = jax.ShapeDtypeStruct((16, ROWS, 128), F32)
    return pl.pallas_call(
        order_kernel,
        out_shape=(jax.ShapeDtypeStruct((2, ROWS), jnp.int32), by_lane, by_lane, by_lane),
        in_specs=[pl.BlockSpec(memory_space=pltpu.SMEM), vmem, there, there, there],
        out_specs=(vmem,) * 4,
        scratch_shapes=[
            pltpu.VMEM((3, ROWS, LENGTH), F32),
            pltpu.VMEM((LENGTH, ROWS), F32),
            pltpu.VMEM((8, 128), F32),
            pltpu.VMEM((3, 8, 128), F32),
            pltpu.SemaphoreType.DMA((3,)),
            pltpu.SemaphoreType.DMA((3,)),
            pltpu.SemaphoreType.DMA((3,)),
        ],
        compiler_params=pltpu.CompilerParams(collective_id=1, has_side_effects=True, vmem_limit_bytes=50 << 20),
        name="order",
    )(lookup, extent, d, t, v)


def band_kernel(table, d_ref, t_ref, v_ref, tau_ref, edge_ref, W, C, NB, N4, Q, M, Zb, S, E):
    lane = lax.broadcasted_iota(jnp.int32, (8, 128), 1)
    sub = lax.broadcasted_iota(jnp.int32, (8, 128), 0)
    zero = jnp.zeros((8, 128), F32)

    def gather(g, _):
        at = pl.ds(pl.multiple_of(g * 16, 16), 16)
        for i in range(8):
            y = table[0, g * 8 + i]
            W[at, i : i + 1, :] = d_ref[:, pl.ds(y, 1), :]
            NB[at, i : i + 1, :] = t_ref[:, pl.ds(y, 1), :]
            C[at, i : i + 1, :] = v_ref[:, pl.ds(y, 1), :]
        return 0

    lax.fori_loop(0, GROUPS, gather, 0)

    def prep(g, _):
        for t in range(16):
            a = g * 16 + t
            warmth = NB[a]
            contrast = W[a]
            nb = (-LOG2E / 169.0) / warmth
            C[a] = 0.5 * (C[a] + float(t))
            NB[a] = nb
            N4[a] = 4.0 * nb
            Q[a] = jnp.exp2(nb + nb)
            W[a] = ((0.3 / 13.0) * jnp.exp2(-1.2 * jnp.log2(warmth))) * (contrast * contrast)
            S[a] = zero
            E[a] = zero
        return 0

    lax.fori_loop(0, GROUPS, prep, 0)

    def group(g, _):
        hv = zero
        for i in range(8):
            hv = jnp.where(sub == i, table[1, g * 8 + i].astype(F32), hv)
        kout = lax.div(table[1, g * 8 + 7] + 15, 16)
        kin = lax.div(table[1, g * 8] - 15, 16)
        base = g * 16
        for r in range(16):
            Zb[1, r] = zero

        def place(dst, sk):
            shift = lax.rem(sk + 128, 128)
            inside = jnp.logical_and(lane >= sk, lane < sk + 128)
            for r in range(16):
                z = pltpu.roll(Zb[1 - dst, r], shift, 1)
                S[base + r] = S[base + r] + jnp.where(inside, z, 0.0)
                E[base + r] = E[base + r] + jnp.where(inside, 0.0, z)

        def cells(Z, kf, masked):
            for s in range(16):
                nb = NB[base + s]
                x = kf - C[base + s]
                m2 = N4[base + s] * x
                A = W[base + s] * jnp.exp2(m2 * x)
                R = jnp.exp2(m2 + nb)
                U = jnp.exp2(nb - m2)
                q = Q[base + s]

                def add(r, G):
                    term = G * M[r - s + 15] if masked else G
                    Z[r] = term if Z[r] is None else Z[r] + term

                add(8, A)
                G = H = A
                for i in range(1, 9):
                    H = H * U
                    add(8 - i, H)
                    if i < 8:
                        G = G * R
                        add(8 + i, G)
                    if i < 7:
                        R = R * q
                    if i < 8:
                        U = U * q

        def step(side, sk, before, dst):
            if side:
                hk = hv - (16 * side * sk).astype(F32)
                for i in range(31):
                    M[i] = jnp.where(hk >= float(side * (i - 15)), 1.0, 0.0)
            Z = [None] * 16
            place(dst, before)
            cells(Z, (8 * sk + 4).astype(F32), side)
            for r in range(16):
                Zb[dst, r] = Z[r]

        def edge_step(side, where, n, carry):
            before, dst = carry
            sk = where(n)
            step(side, sk, before, dst)
            return sk, 1 - dst

        def two_steps(n, carry):
            before, dst = carry
            one = jnp.where(2 * n < kin, 2 * n - kin, 2 * kin - 2 * n)
            two = jnp.where(2 * n + 1 < kin, 2 * n + 1 - kin, 2 * kin - 2 * n - 1)
            step(0, one, before, dst)
            step(0, two, one, 1 - dst)
            return two, dst

        carry = (jnp.int32(0), jnp.int32(0))
        carry = lax.fori_loop(0, kout - kin, functools.partial(edge_step, -1, lambda n: n - kout), carry)
        carry = lax.fori_loop(0, kout - kin, functools.partial(edge_step, 1, lambda n: kout - n), carry)
        carry = lax.fori_loop(0, kin, two_steps, carry)
        carry = lax.fori_loop(kin, kin + 1, functools.partial(edge_step, 0, lambda n: jnp.int32(0)), carry)
        fin = 1 - carry[1]
        for r in range(16):
            S[base + r] = S[base + r] + Zb[fin, r]
        return 0

    lax.fori_loop(0, GROUPS, group, 0)

    def scatter(g, _):
        at = pl.ds(pl.multiple_of(g * 16, 16), 16)
        for i in range(8):
            y = table[0, g * 8 + i]
            tau_ref[:, pl.ds(y, 1), :] = S[at, i : i + 1, :]
            edge_ref[:, pl.ds(y, 1), :] = E[at, i : i + 1, :]
        return 0

    lax.fori_loop(0, GROUPS, scatter, 0)

def band_depth(order, d, t, v):
    whole = pl.BlockSpec((16, ROWS, 128), lambda i, *_: (0, 0, 0))
    table = pltpu.VMEM((GROUPS * 16, 8, 128), F32)
    return pl.pallas_call(
        band_kernel,
        out_shape=(jax.ShapeDtypeStruct((16, ROWS, 128), F32),) * 2,
        grid_spec=pltpu.PrefetchScalarGridSpec(
            num_scalar_prefetch=1, grid=(1,), in_specs=[whole] * 3, out_specs=[whole] * 2,
            scratch_shapes=[table] * 5 + [pltpu.VMEM((31, 8, 128), F32), pltpu.VMEM((2, 16, 8, 128), F32), table, table],
        ),
        compiler_params=pltpu.CompilerParams(vmem_limit_bytes=24 << 20),
        name="band",
    )(order, d, t, v)


def share_kernel(tau, edge, got, sums_out, right, left, from_left, from_right, cells, flux, relay, part, parts, local_sum, sums,
                 edge_send, edge_recv, a_send, a_recv, b_send, b_recv, p_send, p_recv, q_send, q_recv):
    seg, los = lax.axis_index("seg"), lax.axis_index("los")
    y, zh, x = lax.div(seg, 8), lax.rem(lax.div(seg, 4), 2), lax.rem(seg, 4)
    zl, core = lax.div(los, 2), lax.rem(los, 2)
    after, before = lax.rem(los + 1, LOSS), lax.rem(los + LOSS - 1, LOSS)
    me = zh * 4 + los

    def column(d):
        h = 1 - zh if d & 4 else zh
        l = (1 - zl if d & 2 else zl) * 2 + (1 - core if d & 1 else core)
        return h, l

    def plane(dy, dx):
        return lax.rem(y + dy, 4) * 8 + zh * 4 + lax.rem(x + dx, 4)

    barrier = pltpu.get_barrier_semaphore()

    def signal(s, l):
        pl.semaphore_signal(barrier, inc=1, device_id=(s, l), device_id_type=MESH)

    for d in range(1, 8):
        h, l = column(d)
        signal(y * 8 + h * 4 + x, l)
    for i in range(1, 16):
        signal(plane(i // 4, i % 4), los)
    for i in range(16):
        block = edge[i].T
        right[pl.ds(i, 32, stride=16), :] = block[0:32]
        left[pl.ds(i, 32, stride=16), :] = block[96:128]
    pl.semaphore_wait(barrier, 22)

    def remote(src, dst, send, recv, s, l):
        return pltpu.make_async_remote_copy(
            src_ref=src, dst_ref=dst, send_sem=send, recv_sem=recv, device_id=(s, l), device_id_type=MESH
        )

    edges = [
        remote(right, from_left, edge_send.at[0], edge_recv.at[0], seg, after),
        remote(left, from_right, edge_send.at[1], edge_recv.at[1], seg, before),
    ]
    for copy in edges:
        copy.start()
    for i in range(16):
        cells[pl.ds(i, 128, stride=16), :] = tau[i].T

    def depth_of(m):
        return cells[m * 128 : (m + 1) * 128]

    def take_flux(m, depth):
        value = jnp.exp(-depth)
        flux[:, m * 128 : (m + 1) * 128] = value.T
        return jnp.sum(value.reshape(16, 8, 128), axis=0)

    total = jnp.zeros((8, 128), F32)
    for m in range(4, 12):
        total = total + take_flux(m, depth_of(m))
    for copy in edges:
        copy.wait_recv()
    for m in range(4):
        total = total + take_flux(m, depth_of(m) + from_left[m * 128 : (m + 1) * 128])
        total = total + take_flux(m + 12, depth_of(m + 12) + from_right[m * 128 : (m + 1) * 128])
    part[...] = total

    def a_part(d):
        h, l = column(d)
        return flux.at[pl.ds(pl.multiple_of(l * 32, 32), 32), pl.ds(pl.multiple_of(h * 1024, 1024), 1024)]

    def a_copy(d):
        h, l = column(d)
        return remote(a_part(d), relay.at[me], a_send.at[d], a_recv.at[me], y * 8 + h * 4 + x, l)

    def a_arrival(d):
        h, l = column(d)
        return remote(a_part(d), relay.at[h * 4 + l], a_send.at[d], a_recv.at[h * 4 + l], y * 8 + h * 4 + x, l)

    def p_copy(d):
        h, l = column(d)
        return remote(part, parts.at[d - 1], p_send.at[d - 1], p_recv.at[d - 1], y * 8 + h * 4 + x, l)

    for d in range(1, 8):
        p_copy(d).start()
    keep = pltpu.make_async_copy(a_part(0), relay.at[me], a_recv.at[me])
    for d in (4, 2, 6, 5, 3, 7, 1):
        a_copy(d).start()
    keep.start()

    total = part[...]
    for d in range(1, 8):
        p_copy(d).wait_recv()
        total = total + parts[d - 1]
    local_sum[...] = total

    def q_copy(i):
        return remote(local_sum, sums.at[i - 1], q_send.at[i - 1], q_recv.at[i - 1], plane(i // 4, i % 4), los)

    for i in range(1, 16):
        q_copy(i).start()

    def b_part(d, j):
        h, l = column(d)
        to = lax.rem(x + j, 4)
        return relay.at[h * 4 + l, :, pl.ds(pl.multiple_of(to * WIDE, WIDE), WIDE)]

    def b_copy(d, j):
        h, l = column(d)
        slot = y * 8 + h * 4 + x
        return remote(b_part(d, j), got.at[slot], b_send.at[d, j], b_recv.at[slot],
                      l * 8 + zh * 4 + lax.rem(x + j, 4), los)

    def b_keep(d):
        h, l = column(d)
        slot = y * 8 + h * 4 + x
        return pltpu.make_async_copy(b_part(d, 0), got.at[slot], b_recv.at[slot])

    def stays(d):
        return column(d)[1] == y

    def leaves(d):
        return column(d)[1] != y

    for d in (0, 1, 2, 6, 3, 7, 4, 5):
        if d == 0:
            keep.wait()
        else:
            a_arrival(d).wait_recv()
        for j in (2, 1, 3):
            b_copy(d, j).start()

        @pl.when(leaves(d))
        def _():
            b_copy(d, 0).start()

        @pl.when(stays(d))
        def _():
            b_keep(d).start()

    for i in range(1, 16):
        q_copy(i).wait_recv()
        total = total + sums[i - 1]
    sums_out[...] = total

    def take(s, _):
        ys, xs = lax.div(s, 8), lax.rem(s, 4)
        here = jnp.logical_and(ys == y, xs == x)

        @pl.when(jnp.logical_not(here))
        def _():
            remote(relay.at[0, :, pl.ds(0, WIDE)], got.at[s], b_send.at[0, 1], b_recv.at[s],
                   ys * 8 + zh * 4 + xs, los).wait_recv()

        @pl.when(here)
        def _():
            pltpu.make_async_copy(relay.at[0, :, pl.ds(0, WIDE)], got.at[s], b_recv.at[s]).wait()
        return 0

    lax.fori_loop(0, SEGS, take, 0)

    for copy in edges:
        copy.wait_send()
    for d in range(1, 8):
        a_copy(d).wait_send()
        p_copy(d).wait_send()
    for i in range(1, 16):
        q_copy(i).wait_send()
    for d in range(8):
        for j in (1, 2, 3):
            b_copy(d, j).wait_send()

        @pl.when(leaves(d))
        def _():
            b_copy(d, 0).wait_send()


def share(tau, edge):
    vmem = pl.BlockSpec(memory_space=pltpu.VMEM)
    dma = pltpu.SemaphoreType.DMA
    side = pltpu.VMEM((REACH, ROWS), F32)
    return pl.pallas_call(
        share_kernel,
        out_shape=(jax.ShapeDtypeStruct((SEGS, 32, WIDE), F32), jax.ShapeDtypeStruct((8, 128), F32)),
        in_specs=[vmem] * 2,
        out_specs=(pl.BlockSpec(memory_space=pl.ANY), vmem),
        scratch_shapes=[
            side,
            side,
            side,
            side,
            pltpu.VMEM((LENGTH, ROWS), F32),
            pltpu.VMEM((ROWS, LENGTH), F32),
            pltpu.VMEM((8, 32, 1024), F32),
            pltpu.VMEM((8, 128), F32),
            pltpu.VMEM((7, 8, 128), F32),
            pltpu.VMEM((8, 128), F32),
            pltpu.VMEM((15, 8, 128), F32),
            dma((2,)),
            dma((2,)),
            dma((8,)),
            dma((8,)),
            dma((8, 4)),
            dma((SEGS,)),
            dma((7,)),
            dma((7,)),
            dma((15,)),
            dma((15,)),
        ],
        compiler_params=pltpu.CompilerParams(collective_id=0, has_side_effects=True, vmem_limit_bytes=12 << 20),
        name="share",
    )(tau, edge)


def finish_kernel(lookup, got, sums, flux):
    scale = CELLS / jnp.sum(sums[...], axis=(0, 1), keepdims=True)

    def row(k, _):
        flux[k] = got[lookup[k]] * scale
        return 0

    lax.fori_loop(0, SEGS, row, 0)


def finish(lookup, got, sums):
    vmem = pl.BlockSpec(memory_space=pltpu.VMEM)
    return pl.pallas_call(
        finish_kernel,
        out_shape=jax.ShapeDtypeStruct((SEGS, 32, WIDE), F32),
        in_specs=[pl.BlockSpec(memory_space=pltpu.SMEM), vmem, vmem],
        out_specs=vmem,
        compiler_params=pltpu.CompilerParams(vmem_limit_bytes=8 << 20),
        name="finish",
    )(lookup, got, sums)


def per_device(contrast, warmth, velocity, semi_extent, lookup):
    shape = (ROWS, LENGTH)
    order, d, t, v = sightline_order(
        lookup, semi_extent, contrast.reshape(shape), warmth.reshape(shape), velocity.reshape(shape)
    )

    tau, edge = band_depth(order, d, t, v)
    got, sums = share(tau, edge)
    return finish(lookup, got, sums)


def solution(mesh):
    return jax.shard_map(
        per_device,
        mesh=mesh,
        in_specs=(P("seg", None, "los"), P("seg", None, "los"), P("seg", None, "los"), P(None, "los"), P()),
        out_specs=P(None, "los", "seg"),
        check_vma=False,
    )
```

```python
import functools

import jax
import jax.numpy as jnp
from jax import lax
from jax.experimental import pallas as pl
from jax.experimental.pallas import tpu as pltpu
from jax.sharding import PartitionSpec as P

LOG2E = 1.4426950408889634
ROWS = 128
LENGTH = 2048
GROUPS = ROWS // 8
REACH = 512
SEGS, LOSS = 32, 4
WIDE = 256
CELLS = 33554432.0
MESH = pl.DeviceIdType.MESH
F32 = jnp.float32


def order_kernel(lookup, extent, d, t, v, order, d_out, t_out, v_out, fields, cells, tile, tiles, load, send, recv):
    loads = [pltpu.make_async_copy(ref, fields.at[n], load.at[n]) for n, ref in enumerate((d, t, v))]
    for copy in loads:
        copy.start()
    seg, los = lax.axis_index("seg"), lax.axis_index("los")
    barrier = pltpu.get_barrier_semaphore()
    for j in range(1, LOSS):
        pl.semaphore_signal(barrier, inc=1, device_id=(seg, lax.rem(los + j, LOSS)), device_id_type=MESH)

    def turn(n):
        loads[n].wait()

        for m in range(16):
            cells[m * 128 : (m + 1) * 128] = fields[n, :, m * 128 : (m + 1) * 128].T
        for i in range(16):
            (d_out, t_out, v_out)[n][i] = cells[pl.ds(i, 128, stride=16), :].T

    turn(0)
    pl.semaphore_wait(barrier, LOSS - 1)
    row = jnp.int32(0)
    for i in range(SEGS):
        row = jnp.where(lookup[i] == seg, i, row)
    tile[...] = jnp.zeros((8, 128), F32)
    tile[0:1, 0:32] = extent[pl.ds(row, 1), :].astype(F32)
    copies = [
        pltpu.make_async_remote_copy(
            src_ref=tile, dst_ref=tiles.at[j - 1], send_sem=send.at[j - 1], recv_sem=recv.at[j - 1],
            device_id=(seg, lax.rem(los + j, LOSS)), device_id_type=MESH,
        )
        for j in range(1, LOSS)
    ]
    for copy in copies:
        copy.start()
    turn(1)
    turn(2)
    part = lax.broadcasted_iota(jnp.int32, (1, 128), 1) // 32
    for copy in copies:
        copy.wait_recv()
    h = jnp.zeros((1, 128), F32)
    for j in range(LOSS):
        values = (tile if j == 0 else tiles.at[j - 1])[0:1, :]
        owner = lax.rem(los + LOSS - j, LOSS)
        for l in range(LOSS):
            h = h + jnp.where(jnp.logical_and(part == l, owner == l), pltpu.roll(values, 32 * l, 1) if l else values, 0.0)
    i = lax.broadcasted_iota(jnp.int32, (128, 128), 0)
    j = lax.broadcasted_iota(jnp.int32, (128, 128), 1)
    across = jnp.broadcast_to(h, (128, 128))
    down = jnp.sum(jnp.where(i == j, across, 0.0), axis=1, keepdims=True)
    below = jnp.logical_or(across < down, jnp.logical_and(across == down, j < i))
    rank = jnp.sum(jnp.where(below, 1.0, 0.0), axis=1, keepdims=True)
    hot = rank == j.astype(F32)
    order[0:1, :] = jnp.sum(jnp.where(hot, i.astype(F32), 0.0), axis=0, keepdims=True).astype(jnp.int32)
    order[1:2, :] = jnp.sum(jnp.where(hot, down, 0.0), axis=0, keepdims=True).astype(jnp.int32)
    for copy in copies:
        copy.wait_send()


def sightline_order(lookup, extent, d, t, v):
    vmem = pl.BlockSpec(memory_space=pltpu.VMEM)
    there = pl.BlockSpec(memory_space=pl.ANY)
    by_lane = jax.ShapeDtypeStruct((16, ROWS, 128), F32)
    return pl.pallas_call(
        order_kernel,
        out_shape=(jax.ShapeDtypeStruct((2, ROWS), jnp.int32), by_lane, by_lane, by_lane),
        in_specs=[pl.BlockSpec(memory_space=pltpu.SMEM), vmem, there, there, there],
        out_specs=(vmem,) * 4,
        scratch_shapes=[
            pltpu.VMEM((3, ROWS, LENGTH), F32),
            pltpu.VMEM((LENGTH, ROWS), F32),
            pltpu.VMEM((8, 128), F32),
            pltpu.VMEM((3, 8, 128), F32),
            pltpu.SemaphoreType.DMA((3,)),
            pltpu.SemaphoreType.DMA((3,)),
            pltpu.SemaphoreType.DMA((3,)),
        ],
        compiler_params=pltpu.CompilerParams(collective_id=1, has_side_effects=True, vmem_limit_bytes=50 << 20),
        name="order",
    )(lookup, extent, d, t, v)


def band_kernel(table, d_ref, t_ref, v_ref, tau_ref, edge_ref, W, C, NB, N4, Q, M, Zb, S, E):
    lane = lax.broadcasted_iota(jnp.int32, (8, 128), 1)
    sub = lax.broadcasted_iota(jnp.int32, (8, 128), 0)
    zero = jnp.zeros((8, 128), F32)

    def gather(g, _):
        at = pl.ds(pl.multiple_of(g * 16, 16), 16)
        for i in range(8):
            y = table[0, g * 8 + i]
            W[at, i : i + 1, :] = d_ref[:, pl.ds(y, 1), :]
            NB[at, i : i + 1, :] = t_ref[:, pl.ds(y, 1), :]
            C[at, i : i + 1, :] = v_ref[:, pl.ds(y, 1), :]
        return 0

    lax.fori_loop(0, GROUPS, gather, 0)

    def prep(g, _):
        for t in range(16):
            a = g * 16 + t
            warmth = NB[a]
            contrast = W[a]
            nb = (-LOG2E / 169.0) / warmth
            C[a] = 0.5 * (C[a] + float(t))
            NB[a] = nb
            N4[a] = 4.0 * nb
            Q[a] = jnp.exp2(nb + nb)
            W[a] = ((0.3 / 13.0) * jnp.exp2(-1.2 * jnp.log2(warmth))) * (contrast * contrast)
            S[a] = zero
            E[a] = zero
        return 0

    lax.fori_loop(0, GROUPS, prep, 0)

    def group(g, _):
        hv = zero
        for i in range(8):
            hv = jnp.where(sub == i, table[1, g * 8 + i].astype(F32), hv)
        kout = lax.div(table[1, g * 8 + 7] + 15, 16)
        kin = lax.div(table[1, g * 8] - 15, 16)
        base = g * 16
        for r in range(16):
            Zb[1, r] = zero

        def place(dst, sk):
            shift = lax.rem(sk + 128, 128)
            inside = jnp.logical_and(lane >= sk, lane < sk + 128)
            for r in range(16):
                z = pltpu.roll(Zb[1 - dst, r], shift, 1)
                S[base + r] = S[base + r] + jnp.where(inside, z, 0.0)
                E[base + r] = E[base + r] + jnp.where(inside, 0.0, z)

        def cells(Z, kf, masked):
            for s in range(16):
                nb = NB[base + s]
                x = kf - C[base + s]
                m2 = N4[base + s] * x
                A = W[base + s] * jnp.exp2(m2 * x)
                R = jnp.exp2(m2 + nb)
                U = jnp.exp2(nb - m2)
                q = Q[base + s]

                def add(r, G):
                    term = G * M[r - s + 15] if masked else G
                    Z[r] = term if Z[r] is None else Z[r] + term

                add(8, A)
                G = H = A
                for i in range(1, 9):
                    H = H * U
                    add(8 - i, H)
                    if i < 8:
                        G = G * R
                        add(8 + i, G)
                    if i < 7:
                        R = R * q
                    if i < 8:
                        U = U * q

        def step(side, sk, before, dst):
            if side:
                hk = hv - (16 * side * sk).astype(F32)
                for i in range(31):
                    M[i] = jnp.where(hk >= float(side * (i - 15)), 1.0, 0.0)
            Z = [None] * 16
            place(dst, before)
            cells(Z, (8 * sk + 4).astype(F32), side)
            for r in range(16):
                Zb[dst, r] = Z[r]

        def edge_step(side, where, n, carry):
            before, dst = carry
            sk = where(n)
            step(side, sk, before, dst)
            return sk, 1 - dst

        def two_steps(n, carry):
            before, dst = carry
            one = jnp.where(2 * n < kin, 2 * n - kin, 2 * kin - 2 * n)
            two = jnp.where(2 * n + 1 < kin, 2 * n + 1 - kin, 2 * kin - 2 * n - 1)
            step(0, one, before, dst)
            step(0, two, one, 1 - dst)
            return two, dst

        carry = (jnp.int32(0), jnp.int32(0))
        carry = lax.fori_loop(0, kout - kin, functools.partial(edge_step, -1, lambda n: n - kout), carry)
        carry = lax.fori_loop(0, kout - kin, functools.partial(edge_step, 1, lambda n: kout - n), carry)
        carry = lax.fori_loop(0, kin, two_steps, carry)
        carry = lax.fori_loop(kin, kin + 1, functools.partial(edge_step, 0, lambda n: jnp.int32(0)), carry)
        fin = 1 - carry[1]
        for r in range(16):
            S[base + r] = S[base + r] + Zb[fin, r]
        return 0

    lax.fori_loop(0, GROUPS, group, 0)

    def scatter(g, _):
        at = pl.ds(pl.multiple_of(g * 16, 16), 16)
        for i in range(8):
            y = table[0, g * 8 + i]
            tau_ref[:, pl.ds(y, 1), :] = S[at, i : i + 1, :]
            edge_ref[:, pl.ds(y, 1), :] = E[at, i : i + 1, :]
        return 0

    lax.fori_loop(0, GROUPS, scatter, 0)

def band_depth(order, d, t, v):
    whole = pl.BlockSpec((16, ROWS, 128), lambda i, *_: (0, 0, 0))
    table = pltpu.VMEM((GROUPS * 16, 8, 128), F32)
    return pl.pallas_call(
        band_kernel,
        out_shape=(jax.ShapeDtypeStruct((16, ROWS, 128), F32),) * 2,
        grid_spec=pltpu.PrefetchScalarGridSpec(
            num_scalar_prefetch=1, grid=(1,), in_specs=[whole] * 3, out_specs=[whole] * 2,
            scratch_shapes=[table] * 5 + [pltpu.VMEM((31, 8, 128), F32), pltpu.VMEM((2, 16, 8, 128), F32), table, table],
        ),
        compiler_params=pltpu.CompilerParams(vmem_limit_bytes=24 << 20),
        name="band",
    )(order, d, t, v)


def share_kernel(tau, edge, got, sums_out, right, left, from_left, from_right, cells, flux, relay, part, parts, local_sum, sums,
                 edge_send, edge_recv, a_send, a_recv, b_send, b_recv, p_send, p_recv, q_send, q_recv):
    seg, los = lax.axis_index("seg"), lax.axis_index("los")
    y, zh, x = lax.div(seg, 8), lax.rem(lax.div(seg, 4), 2), lax.rem(seg, 4)
    zl, core = lax.div(los, 2), lax.rem(los, 2)
    after, before = lax.rem(los + 1, LOSS), lax.rem(los + LOSS - 1, LOSS)
    me = zh * 4 + los

    def column(d):
        h = 1 - zh if d & 4 else zh
        l = (1 - zl if d & 2 else zl) * 2 + (1 - core if d & 1 else core)
        return h, l

    def plane(dy, dx):
        return lax.rem(y + dy, 4) * 8 + zh * 4 + lax.rem(x + dx, 4)

    barrier = pltpu.get_barrier_semaphore()

    def signal(s, l):
        pl.semaphore_signal(barrier, inc=1, device_id=(s, l), device_id_type=MESH)

    for d in range(1, 8):
        h, l = column(d)
        signal(y * 8 + h * 4 + x, l)
    for i in range(1, 16):
        signal(plane(i // 4, i % 4), los)
    for i in range(16):
        block = edge[i].T
        right[pl.ds(i, 32, stride=16), :] = block[0:32]
        left[pl.ds(i, 32, stride=16), :] = block[96:128]
    pl.semaphore_wait(barrier, 22)

    def remote(src, dst, send, recv, s, l):
        return pltpu.make_async_remote_copy(
            src_ref=src, dst_ref=dst, send_sem=send, recv_sem=recv, device_id=(s, l), device_id_type=MESH
        )

    edges = [
        remote(right, from_left, edge_send.at[0], edge_recv.at[0], seg, after),
        remote(left, from_right, edge_send.at[1], edge_recv.at[1], seg, before),
    ]
    for copy in edges:
        copy.start()
    for i in range(16):
        cells[pl.ds(i, 128, stride=16), :] = tau[i].T

    def depth_of(m):
        return cells[m * 128 : (m + 1) * 128]

    def take_flux(m, depth):
        value = jnp.exp(-depth)
        flux[:, m * 128 : (m + 1) * 128] = value.T
        return jnp.sum(value.reshape(16, 8, 128), axis=0)

    total = jnp.zeros((8, 128), F32)
    for m in range(4, 12):
        total = total + take_flux(m, depth_of(m))
    for copy in edges:
        copy.wait_recv()
    for m in range(4):
        total = total + take_flux(m, depth_of(m) + from_left[m * 128 : (m + 1) * 128])
        total = total + take_flux(m + 12, depth_of(m + 12) + from_right[m * 128 : (m + 1) * 128])
    part[...] = total

    def a_part(d):
        h, l = column(d)
        return flux.at[pl.ds(pl.multiple_of(l * 32, 32), 32), pl.ds(pl.multiple_of(h * 1024, 1024), 1024)]

    def a_copy(d):
        h, l = column(d)
        return remote(a_part(d), relay.at[me], a_send.at[d], a_recv.at[me], y * 8 + h * 4 + x, l)

    def a_arrival(d):
        h, l = column(d)
        return remote(a_part(d), relay.at[h * 4 + l], a_send.at[d], a_recv.at[h * 4 + l], y * 8 + h * 4 + x, l)

    def p_copy(d):
        h, l = column(d)
        return remote(part, parts.at[d - 1], p_send.at[d - 1], p_recv.at[d - 1], y * 8 + h * 4 + x, l)

    for d in range(1, 8):
        p_copy(d).start()
    keep = pltpu.make_async_copy(a_part(0), relay.at[me], a_recv.at[me])
    for d in (2, 4, 6, 3, 5, 7, 1):
        a_copy(d).start()
    keep.start()

    total = part[...]
    for d in range(1, 8):
        p_copy(d).wait_recv()
        total = total + parts[d - 1]
    local_sum[...] = total

    def q_copy(i):
        return remote(local_sum, sums.at[i - 1], q_send.at[i - 1], q_recv.at[i - 1], plane(i // 4, i % 4), los)

    for i in range(1, 16):
        q_copy(i).start()

    def b_part(d, j):
        h, l = column(d)
        to = lax.rem(x + j, 4)
        return relay.at[h * 4 + l, :, pl.ds(pl.multiple_of(to * WIDE, WIDE), WIDE)]

    def b_copy(d, j):
        h, l = column(d)
        slot = y * 8 + h * 4 + x
        return remote(b_part(d, j), got.at[slot], b_send.at[d, j], b_recv.at[slot],
                      l * 8 + zh * 4 + lax.rem(x + j, 4), los)

    def b_keep(d):
        h, l = column(d)
        slot = y * 8 + h * 4 + x
        return pltpu.make_async_copy(b_part(d, 0), got.at[slot], b_recv.at[slot])

    def stays(d):
        return column(d)[1] == y

    def leaves(d):
        return column(d)[1] != y

    for d in (0, 1, 2, 4, 6, 3, 5, 7):
        if d == 0:
            keep.wait()
        else:
            a_arrival(d).wait_recv()
        for j in (2, 1, 3):
            b_copy(d, j).start()

        @pl.when(leaves(d))
        def _():
            b_copy(d, 0).start()

        @pl.when(stays(d))
        def _():
            b_keep(d).start()

    for i in range(1, 16):
        q_copy(i).wait_recv()
        total = total + sums[i - 1]
    sums_out[...] = total

    def take(s, _):
        ys, xs = lax.div(s, 8), lax.rem(s, 4)
        here = jnp.logical_and(ys == y, xs == x)

        @pl.when(jnp.logical_not(here))
        def _():
            remote(relay.at[0, :, pl.ds(0, WIDE)], got.at[s], b_send.at[0, 1], b_recv.at[s],
                   ys * 8 + zh * 4 + xs, los).wait_recv()

        @pl.when(here)
        def _():
            pltpu.make_async_copy(relay.at[0, :, pl.ds(0, WIDE)], got.at[s], b_recv.at[s]).wait()
        return 0

    lax.fori_loop(0, SEGS, take, 0)

    for copy in edges:
        copy.wait_send()
    for d in range(1, 8):
        a_copy(d).wait_send()
        p_copy(d).wait_send()
    for i in range(1, 16):
        q_copy(i).wait_send()
    for d in range(8):
        for j in (1, 2, 3):
            b_copy(d, j).wait_send()

        @pl.when(leaves(d))
        def _():
            b_copy(d, 0).wait_send()


def share(tau, edge):
    vmem = pl.BlockSpec(memory_space=pltpu.VMEM)
    dma = pltpu.SemaphoreType.DMA
    side = pltpu.VMEM((REACH, ROWS), F32)
    return pl.pallas_call(
        share_kernel,
        out_shape=(jax.ShapeDtypeStruct((SEGS, 32, WIDE), F32), jax.ShapeDtypeStruct((8, 128), F32)),
        in_specs=[vmem] * 2,
        out_specs=(pl.BlockSpec(memory_space=pl.ANY), vmem),
        scratch_shapes=[
            side,
            side,
            side,
            side,
            pltpu.VMEM((LENGTH, ROWS), F32),
            pltpu.VMEM((ROWS, LENGTH), F32),
            pltpu.VMEM((8, 32, 1024), F32),
            pltpu.VMEM((8, 128), F32),
            pltpu.VMEM((7, 8, 128), F32),
            pltpu.VMEM((8, 128), F32),
            pltpu.VMEM((15, 8, 128), F32),
            dma((2,)),
            dma((2,)),
            dma((8,)),
            dma((8,)),
            dma((8, 4)),
            dma((SEGS,)),
            dma((7,)),
            dma((7,)),
            dma((15,)),
            dma((15,)),
        ],
        compiler_params=pltpu.CompilerParams(collective_id=0, has_side_effects=True, vmem_limit_bytes=12 << 20),
        name="share",
    )(tau, edge)


def finish_kernel(lookup, got, sums, flux):
    scale = CELLS / jnp.sum(sums[...], axis=(0, 1), keepdims=True)

    def row(k, _):
        flux[k] = got[lookup[k]] * scale
        return 0

    lax.fori_loop(0, SEGS, row, 0)


def finish(lookup, got, sums):
    vmem = pl.BlockSpec(memory_space=pltpu.VMEM)
    return pl.pallas_call(
        finish_kernel,
        out_shape=jax.ShapeDtypeStruct((SEGS, 32, WIDE), F32),
        in_specs=[pl.BlockSpec(memory_space=pltpu.SMEM), vmem, vmem],
        out_specs=vmem,
        compiler_params=pltpu.CompilerParams(vmem_limit_bytes=8 << 20),
        name="finish",
    )(lookup, got, sums)


def per_device(contrast, warmth, velocity, semi_extent, lookup):
    shape = (ROWS, LENGTH)
    order, d, t, v = sightline_order(
        lookup, semi_extent, contrast.reshape(shape), warmth.reshape(shape), velocity.reshape(shape)
    )

    tau, edge = band_depth(order, d, t, v)
    got, sums = share(tau, edge)
    return finish(lookup, got, sums)


def solution(mesh):
    return jax.shard_map(
        per_device,
        mesh=mesh,
        in_specs=(P("seg", None, "los"), P("seg", None, "los"), P("seg", None, "los"), P(None, "los"), P()),
        out_specs=P(None, "los", "seg"),
        check_vma=False,
    )
```

```python
import functools

import jax
import jax.numpy as jnp
from jax import lax
from jax.experimental import pallas as pl
from jax.experimental.pallas import tpu as pltpu
from jax.sharding import PartitionSpec as P

LOG2E = 1.4426950408889634
ROWS = 128
LENGTH = 2048
GROUPS = ROWS // 8
REACH = 512
SEGS, LOSS = 32, 4
WIDE = 256
CELLS = 33554432.0
MESH = pl.DeviceIdType.MESH
F32 = jnp.float32


def order_kernel(lookup, extent, d, t, v, order, d_out, t_out, v_out, fields, cells, tile, tiles, load, send, recv):
    loads = [pltpu.make_async_copy(ref, fields.at[n], load.at[n]) for n, ref in enumerate((d, t, v))]
    for copy in loads:
        copy.start()
    seg, los = lax.axis_index("seg"), lax.axis_index("los")
    barrier = pltpu.get_barrier_semaphore()
    for j in range(1, LOSS):
        pl.semaphore_signal(barrier, inc=1, device_id=(seg, lax.rem(los + j, LOSS)), device_id_type=MESH)

    def turn(n):
        loads[n].wait()

        for m in range(16):
            cells[m * 128 : (m + 1) * 128] = fields[n, :, m * 128 : (m + 1) * 128].T
        for i in range(16):
            (d_out, t_out, v_out)[n][i] = cells[pl.ds(i, 128, stride=16), :].T

    turn(0)
    pl.semaphore_wait(barrier, LOSS - 1)
    row = jnp.int32(0)
    for i in range(SEGS):
        row = jnp.where(lookup[i] == seg, i, row)
    tile[...] = jnp.zeros((8, 128), F32)
    tile[0:1, 0:32] = extent[pl.ds(row, 1), :].astype(F32)
    copies = [
        pltpu.make_async_remote_copy(
            src_ref=tile, dst_ref=tiles.at[j - 1], send_sem=send.at[j - 1], recv_sem=recv.at[j - 1],
            device_id=(seg, lax.rem(los + j, LOSS)), device_id_type=MESH,
        )
        for j in range(1, LOSS)
    ]
    for copy in copies:
        copy.start()
    turn(1)
    turn(2)
    part = lax.broadcasted_iota(jnp.int32, (1, 128), 1) // 32
    for copy in copies:
        copy.wait_recv()
    h = jnp.zeros((1, 128), F32)
    for j in range(LOSS):
        values = (tile if j == 0 else tiles.at[j - 1])[0:1, :]
        owner = lax.rem(los + LOSS - j, LOSS)
        for l in range(LOSS):
            h = h + jnp.where(jnp.logical_and(part == l, owner == l), pltpu.roll(values, 32 * l, 1) if l else values, 0.0)
    i = lax.broadcasted_iota(jnp.int32, (128, 128), 0)
    j = lax.broadcasted_iota(jnp.int32, (128, 128), 1)
    across = jnp.broadcast_to(h, (128, 128))
    down = jnp.sum(jnp.where(i == j, across, 0.0), axis=1, keepdims=True)
    below = jnp.logical_or(across < down, jnp.logical_and(across == down, j < i))
    rank = jnp.sum(jnp.where(below, 1.0, 0.0), axis=1, keepdims=True)
    hot = rank == j.astype(F32)
    order[0:1, :] = jnp.sum(jnp.where(hot, i.astype(F32), 0.0), axis=0, keepdims=True).astype(jnp.int32)
    order[1:2, :] = jnp.sum(jnp.where(hot, down, 0.0), axis=0, keepdims=True).astype(jnp.int32)
    for copy in copies:
        copy.wait_send()


def sightline_order(lookup, extent, d, t, v):
    vmem = pl.BlockSpec(memory_space=pltpu.VMEM)
    there = pl.BlockSpec(memory_space=pl.ANY)
    by_lane = jax.ShapeDtypeStruct((16, ROWS, 128), F32)
    return pl.pallas_call(
        order_kernel,
        out_shape=(jax.ShapeDtypeStruct((2, ROWS), jnp.int32), by_lane, by_lane, by_lane),
        in_specs=[pl.BlockSpec(memory_space=pltpu.SMEM), vmem, there, there, there],
        out_specs=(vmem,) * 4,
        scratch_shapes=[
            pltpu.VMEM((3, ROWS, LENGTH), F32),
            pltpu.VMEM((LENGTH, ROWS), F32),
            pltpu.VMEM((8, 128), F32),
            pltpu.VMEM((3, 8, 128), F32),
            pltpu.SemaphoreType.DMA((3,)),
            pltpu.SemaphoreType.DMA((3,)),
            pltpu.SemaphoreType.DMA((3,)),
        ],
        compiler_params=pltpu.CompilerParams(collective_id=1, has_side_effects=True, vmem_limit_bytes=50 << 20),
        name="order",
    )(lookup, extent, d, t, v)


def band_kernel(table, d_ref, t_ref, v_ref, tau_ref, edge_ref, W, C, NB, N4, Q, M, Zb, S, E):
    lane = lax.broadcasted_iota(jnp.int32, (8, 128), 1)
    sub = lax.broadcasted_iota(jnp.int32, (8, 128), 0)
    zero = jnp.zeros((8, 128), F32)

    def gather(g, _):
        at = pl.ds(pl.multiple_of(g * 16, 16), 16)
        for i in range(8):
            y = table[0, g * 8 + i]
            W[at, i : i + 1, :] = d_ref[:, pl.ds(y, 1), :]
            NB[at, i : i + 1, :] = t_ref[:, pl.ds(y, 1), :]
            C[at, i : i + 1, :] = v_ref[:, pl.ds(y, 1), :]
        return 0

    lax.fori_loop(0, GROUPS, gather, 0)

    def prep(g, _):
        for t in range(16):
            a = g * 16 + t
            warmth = NB[a]
            contrast = W[a]
            nb = (-LOG2E / 169.0) / warmth
            C[a] = 0.5 * (C[a] + float(t))
            NB[a] = nb
            N4[a] = 4.0 * nb
            Q[a] = jnp.exp2(nb + nb)
            W[a] = ((0.3 / 13.0) * jnp.exp2(-1.2 * jnp.log2(warmth))) * (contrast * contrast)
            S[a] = zero
            E[a] = zero
        return 0

    lax.fori_loop(0, GROUPS, prep, 0)

    def group(g, _):
        hv = zero
        for i in range(8):
            hv = jnp.where(sub == i, table[1, g * 8 + i].astype(F32), hv)
        kout = lax.div(table[1, g * 8 + 7] + 15, 16)
        kin = lax.div(table[1, g * 8] - 15, 16)
        base = g * 16
        for r in range(16):
            Zb[1, r] = zero

        def place(dst, sk):
            shift = lax.rem(sk + 128, 128)
            inside = jnp.logical_and(lane >= sk, lane < sk + 128)
            outside = jnp.logical_not(inside)
            for r in range(16):
                z = pltpu.roll(Zb[1 - dst, r], shift, 1)
                both = jnp.where(inside, S[base + r], E[base + r]) + z
                pltpu.store(S.at[base + r], both, mask=inside)
                pltpu.store(E.at[base + r], both, mask=outside)

        def cells(Z, kf, masked):
            for s in range(16):
                nb = NB[base + s]
                x = kf - C[base + s]
                m2 = N4[base + s] * x
                A = W[base + s] * jnp.exp2(m2 * x)
                R = jnp.exp2(m2 + nb)
                U = jnp.exp2(nb - m2)
                q = Q[base + s]

                def add(r, G):
                    term = G * M[r - s + 15] if masked else G
                    Z[r] = term if Z[r] is None else Z[r] + term

                add(8, A)
                G = H = A
                for i in range(1, 9):
                    H = H * U
                    add(8 - i, H)
                    if i < 8:
                        G = G * R
                        add(8 + i, G)
                    if i < 7:
                        R = R * q
                    if i < 8:
                        U = U * q

        def step(side, sk, before, dst):
            if side:
                hk = hv - (16 * side * sk).astype(F32)
                for i in range(31):
                    M[i] = jnp.where(hk >= float(side * (i - 15)), 1.0, 0.0)
            Z = [None] * 16
            place(dst, before)
            cells(Z, (8 * sk + 4).astype(F32), side)
            for r in range(16):
                Zb[dst, r] = Z[r]

        def edge_step(side, where, n, carry):
            before, dst = carry
            sk = where(n)
            step(side, sk, before, dst)
            return sk, 1 - dst

        def two_steps(n, carry):
            before, dst = carry
            one = jnp.where(2 * n < kin, 2 * n - kin, 2 * kin - 2 * n)
            two = jnp.where(2 * n + 1 < kin, 2 * n + 1 - kin, 2 * kin - 2 * n - 1)
            step(0, one, before, dst)
            step(0, two, one, 1 - dst)
            return two, dst

        carry = (jnp.int32(0), jnp.int32(0))
        carry = lax.fori_loop(0, kout - kin, functools.partial(edge_step, -1, lambda n: n - kout), carry)
        carry = lax.fori_loop(0, kout - kin, functools.partial(edge_step, 1, lambda n: kout - n), carry)
        carry = lax.fori_loop(0, kin, two_steps, carry)
        carry = lax.fori_loop(kin, kin + 1, functools.partial(edge_step, 0, lambda n: jnp.int32(0)), carry)
        fin = 1 - carry[1]
        for r in range(16):
            S[base + r] = S[base + r] + Zb[fin, r]
        return 0

    lax.fori_loop(0, GROUPS, group, 0)

    def scatter(g, _):
        at = pl.ds(pl.multiple_of(g * 16, 16), 16)
        for i in range(8):
            y = table[0, g * 8 + i]
            tau_ref[:, pl.ds(y, 1), :] = S[at, i : i + 1, :]
            edge_ref[:, pl.ds(y, 1), :] = E[at, i : i + 1, :]
        return 0

    lax.fori_loop(0, GROUPS, scatter, 0)

def band_depth(order, d, t, v):
    whole = pl.BlockSpec((16, ROWS, 128), lambda i, *_: (0, 0, 0))
    table = pltpu.VMEM((GROUPS * 16, 8, 128), F32)
    return pl.pallas_call(
        band_kernel,
        out_shape=(jax.ShapeDtypeStruct((16, ROWS, 128), F32),) * 2,
        grid_spec=pltpu.PrefetchScalarGridSpec(
            num_scalar_prefetch=1, grid=(1,), in_specs=[whole] * 3, out_specs=[whole] * 2,
            scratch_shapes=[table] * 5 + [pltpu.VMEM((31, 8, 128), F32), pltpu.VMEM((2, 16, 8, 128), F32), table, table],
        ),
        compiler_params=pltpu.CompilerParams(vmem_limit_bytes=24 << 20),
        name="band",
    )(order, d, t, v)


def share_kernel(tau, edge, got, sums_out, right, left, from_left, from_right, cells, flux, relay, part, parts, local_sum, sums,
                 edge_send, edge_recv, a_send, a_recv, b_send, b_recv, p_send, p_recv, q_send, q_recv):
    seg, los = lax.axis_index("seg"), lax.axis_index("los")
    y, zh, x = lax.div(seg, 8), lax.rem(lax.div(seg, 4), 2), lax.rem(seg, 4)
    zl, core = lax.div(los, 2), lax.rem(los, 2)
    after, before = lax.rem(los + 1, LOSS), lax.rem(los + LOSS - 1, LOSS)
    me = zh * 4 + los

    def column(d):
        h = 1 - zh if d & 4 else zh
        l = (1 - zl if d & 2 else zl) * 2 + (1 - core if d & 1 else core)
        return h, l

    def plane(dy, dx):
        return lax.rem(y + dy, 4) * 8 + zh * 4 + lax.rem(x + dx, 4)

    barrier = pltpu.get_barrier_semaphore()

    def signal(s, l):
        pl.semaphore_signal(barrier, inc=1, device_id=(s, l), device_id_type=MESH)

    for d in range(1, 8):
        h, l = column(d)
        signal(y * 8 + h * 4 + x, l)
    for i in range(1, 16):
        signal(plane(i // 4, i % 4), los)
    for i in range(16):
        block = edge[i].T
        right[pl.ds(i, 32, stride=16), :] = block[0:32]
        left[pl.ds(i, 32, stride=16), :] = block[96:128]
    pl.semaphore_wait(barrier, 22)

    def remote(src, dst, send, recv, s, l):
        return pltpu.make_async_remote_copy(
            src_ref=src, dst_ref=dst, send_sem=send, recv_sem=recv, device_id=(s, l), device_id_type=MESH
        )

    edges = [
        remote(right, from_left, edge_send.at[0], edge_recv.at[0], seg, after),
        remote(left, from_right, edge_send.at[1], edge_recv.at[1], seg, before),
    ]
    for copy in edges:
        copy.start()
    for i in range(16):
        cells[pl.ds(i, 128, stride=16), :] = tau[i].T

    def depth_of(m):
        return cells[m * 128 : (m + 1) * 128]

    def take_flux(m, depth):
        value = jnp.exp(-depth)
        flux[:, m * 128 : (m + 1) * 128] = value.T
        return jnp.sum(value.reshape(16, 8, 128), axis=0)

    total = jnp.zeros((8, 128), F32)
    for m in range(4, 12):
        total = total + take_flux(m, depth_of(m))
    for copy in edges:
        copy.wait_recv()
    for m in range(4):
        total = total + take_flux(m, depth_of(m) + from_left[m * 128 : (m + 1) * 128])
        total = total + take_flux(m + 12, depth_of(m + 12) + from_right[m * 128 : (m + 1) * 128])
    part[...] = total

    def a_part(d):
        h, l = column(d)
        return flux.at[pl.ds(pl.multiple_of(l * 32, 32), 32), pl.ds(pl.multiple_of(h * 1024, 1024), 1024)]

    def a_copy(d):
        h, l = column(d)
        return remote(a_part(d), relay.at[me], a_send.at[d], a_recv.at[me], y * 8 + h * 4 + x, l)

    def a_arrival(d):
        h, l = column(d)
        return remote(a_part(d), relay.at[h * 4 + l], a_send.at[d], a_recv.at[h * 4 + l], y * 8 + h * 4 + x, l)

    def p_copy(d):
        h, l = column(d)
        return remote(part, parts.at[d - 1], p_send.at[d - 1], p_recv.at[d - 1], y * 8 + h * 4 + x, l)

    for d in range(1, 8):
        p_copy(d).start()
    keep = pltpu.make_async_copy(a_part(0), relay.at[me], a_recv.at[me])
    for d in (2, 4, 6, 3, 5, 7, 1):
        a_copy(d).start()
    keep.start()

    total = part[...]
    for d in range(1, 8):
        p_copy(d).wait_recv()
        total = total + parts[d - 1]
    local_sum[...] = total

    def q_copy(i):
        return remote(local_sum, sums.at[i - 1], q_send.at[i - 1], q_recv.at[i - 1], plane(i // 4, i % 4), los)

    for i in range(1, 16):
        q_copy(i).start()

    def b_part(d, j):
        h, l = column(d)
        to = lax.rem(x + j, 4)
        return relay.at[h * 4 + l, :, pl.ds(pl.multiple_of(to * WIDE, WIDE), WIDE)]

    def b_copy(d, j):
        h, l = column(d)
        slot = y * 8 + h * 4 + x
        return remote(b_part(d, j), got.at[slot], b_send.at[d, j], b_recv.at[slot],
                      l * 8 + zh * 4 + lax.rem(x + j, 4), los)

    def b_keep(d):
        h, l = column(d)
        slot = y * 8 + h * 4 + x
        return pltpu.make_async_copy(b_part(d, 0), got.at[slot], b_recv.at[slot])

    def stays(d):
        return column(d)[1] == y

    def leaves(d):
        return column(d)[1] != y

    for d in (0, 1, 2, 4, 6, 3, 5, 7):
        if d == 0:
            keep.wait()
        else:
            a_arrival(d).wait_recv()
        for j in (2, 1, 3):
            b_copy(d, j).start()

        @pl.when(leaves(d))
        def _():
            b_copy(d, 0).start()

        @pl.when(stays(d))
        def _():
            b_keep(d).start()

    for i in range(1, 16):
        q_copy(i).wait_recv()
        total = total + sums[i - 1]
    sums_out[...] = total

    def take(s, _):
        ys, xs = lax.div(s, 8), lax.rem(s, 4)
        here = jnp.logical_and(ys == y, xs == x)

        @pl.when(jnp.logical_not(here))
        def _():
            remote(relay.at[0, :, pl.ds(0, WIDE)], got.at[s], b_send.at[0, 1], b_recv.at[s],
                   ys * 8 + zh * 4 + xs, los).wait_recv()

        @pl.when(here)
        def _():
            pltpu.make_async_copy(relay.at[0, :, pl.ds(0, WIDE)], got.at[s], b_recv.at[s]).wait()
        return 0

    lax.fori_loop(0, SEGS, take, 0)

    for copy in edges:
        copy.wait_send()
    for d in range(1, 8):
        a_copy(d).wait_send()
        p_copy(d).wait_send()
    for i in range(1, 16):
        q_copy(i).wait_send()
    for d in range(8):
        for j in (1, 2, 3):
            b_copy(d, j).wait_send()

        @pl.when(leaves(d))
        def _():
            b_copy(d, 0).wait_send()


def share(tau, edge):
    vmem = pl.BlockSpec(memory_space=pltpu.VMEM)
    dma = pltpu.SemaphoreType.DMA
    side = pltpu.VMEM((REACH, ROWS), F32)
    return pl.pallas_call(
        share_kernel,
        out_shape=(jax.ShapeDtypeStruct((SEGS, 32, WIDE), F32), jax.ShapeDtypeStruct((8, 128), F32)),
        in_specs=[vmem] * 2,
        out_specs=(pl.BlockSpec(memory_space=pl.ANY), vmem),
        scratch_shapes=[
            side,
            side,
            side,
            side,
            pltpu.VMEM((LENGTH, ROWS), F32),
            pltpu.VMEM((ROWS, LENGTH), F32),
            pltpu.VMEM((8, 32, 1024), F32),
            pltpu.VMEM((8, 128), F32),
            pltpu.VMEM((7, 8, 128), F32),
            pltpu.VMEM((8, 128), F32),
            pltpu.VMEM((15, 8, 128), F32),
            dma((2,)),
            dma((2,)),
            dma((8,)),
            dma((8,)),
            dma((8, 4)),
            dma((SEGS,)),
            dma((7,)),
            dma((7,)),
            dma((15,)),
            dma((15,)),
        ],
        compiler_params=pltpu.CompilerParams(collective_id=0, has_side_effects=True, vmem_limit_bytes=12 << 20),
        name="share",
    )(tau, edge)


def finish_kernel(lookup, got, sums, flux):
    scale = CELLS / jnp.sum(sums[...], axis=(0, 1), keepdims=True)

    def row(k, _):
        flux[k] = got[lookup[k]] * scale
        return 0

    lax.fori_loop(0, SEGS, row, 0)


def finish(lookup, got, sums):
    vmem = pl.BlockSpec(memory_space=pltpu.VMEM)
    return pl.pallas_call(
        finish_kernel,
        out_shape=jax.ShapeDtypeStruct((SEGS, 32, WIDE), F32),
        in_specs=[pl.BlockSpec(memory_space=pltpu.SMEM), vmem, vmem],
        out_specs=vmem,
        compiler_params=pltpu.CompilerParams(vmem_limit_bytes=8 << 20),
        name="finish",
    )(lookup, got, sums)


def per_device(contrast, warmth, velocity, semi_extent, lookup):
    shape = (ROWS, LENGTH)
    order, d, t, v = sightline_order(
        lookup, semi_extent, contrast.reshape(shape), warmth.reshape(shape), velocity.reshape(shape)
    )

    tau, edge = band_depth(order, d, t, v)
    got, sums = share(tau, edge)
    return finish(lookup, got, sums)


def solution(mesh):
    return jax.shard_map(
        per_device,
        mesh=mesh,
        in_specs=(P("seg", None, "los"), P("seg", None, "los"), P("seg", None, "los"), P(None, "los"), P()),
        out_specs=P(None, "los", "seg"),
        check_vma=False,
    )
```
